256 devices in a mesh: rows: 64 (over z, x, core), feat: 4 (over y).
Axes of the slice: x: 4, y: 4, z: 8, core: 2. Of those that a mesh axis runs over, the one named last changes fastest.
Arguments:
- features: float32 [131072, 1024], P('rows', 'feat')
- norm_gain: float32 [1024], P('feat'), may hold values from 0.1 to 1.9
- row_counts: int32 [64, 16], P('rows'), may hold values from 1 to 64, 128 in all within a row
- tile_cols: int32 [8192], P('rows'), may hold values from 0 to 1023, as said below
- tile_values: float32 [8192, 128, 128], P('rows'), may hold values from -0.1875 to 0.1875
Outputs:
- normed: float32 [131072, 1024], P('rows', 'feat')
The draws below stay inside these ranges and needn't reach their ends.
Inputs may be any that keep to these rules, and one draw needn't show every extreme that they name: `tile_cols`: node n lies in stripe n // 2048. There are exactly 3 heavy stripes; every device's tiles reference every block of every heavy stripe and every block of its own stripe. Every other block that a device's tiles reference is referenced by one of its tiles only, lies in no heavy stripe, and no two such blocks of one device lie in the same stripe; each device has exactly 45 such blocks. `row_counts`: each device's counts sum to 128.
All inputs are finite; a program needn't handle non-finite values.
Results may differ from the reference program's by a relative error of at most 0.0003.
Values sent between devices are 32-bit elements; how exact they have to be, the bound alone decides.
A program may use at most 128 MiB of HBM per device.

```python
import math
import jax
import jax.numpy as jnp
import numpy as np
from jax import lax

F = 1024
NODE_DEV = 2048
BLOCK = 128
HEAVY = 3
SPARE = 19
BLK_DEV = 16
NODES = 131072
NEED = 45
TILES = 128
MOST = 64
N_ROWS = 64


def shuffle_row(row_key, row_ids):
    return jax.random.permutation(row_key, row_ids)


def owner_ranking(row_key):
    return jax.random.permutation(row_key, N_ROWS)


def build_plan(key):
    base_key = jax.random.fold_in(key, 4242)
    key_heavy, key_rank, key_block, key_spare, key_shuffle = jax.random.split(base_key, 5)
    owner_order = jax.random.permutation(key_heavy, N_ROWS)
    heavy_devs = owner_order[:HEAVY].astype(jnp.int32)
    owner_ids = jnp.arange(N_ROWS, dtype=jnp.int32)
    reader_ids = owner_ids[:, None]
    owner_heavy = jnp.any(owner_ids[:, None] == heavy_devs[None, :], axis=1)
    rank_table = jax.vmap(owner_ranking)(jax.random.split(key_rank, N_ROWS)).astype(jnp.int32)
    blocked = owner_heavy[None, :] | (owner_ids[None, :] == reader_ids)
    scores = rank_table + N_ROWS * blocked.astype(jnp.int32)
    chosen = jnp.argsort(scores, axis=1, stable=True)[:, :NEED].astype(jnp.int32)
    picked = jax.random.randint(key_block, (N_ROWS, NEED), 0, BLK_DEV, dtype=jnp.int32)
    light_ids = chosen * BLK_DEV + picked
    block_ids = jnp.arange(BLK_DEV, dtype=jnp.int32)
    heavy_list = (heavy_devs[:, None] * BLK_DEV + block_ids[None, :]).reshape(-1)
    own_list = reader_ids * BLK_DEV + block_ids[None, :]
    pool_ids = jnp.concatenate([jnp.broadcast_to(heavy_list[None, :], (N_ROWS, HEAVY * BLK_DEV)), own_list], axis=1)
    extra_pick = jax.random.randint(key_spare, (N_ROWS, SPARE), 0, (HEAVY + 1) * BLK_DEV, dtype=jnp.int32)
    extra_ids = jnp.take_along_axis(pool_ids, extra_pick, axis=1)
    every_id = jnp.concatenate([light_ids, pool_ids, extra_ids], axis=1)
    shuffled = jax.vmap(shuffle_row)(jax.random.split(key_shuffle, N_ROWS), every_id)
    return shuffled.astype(jnp.int32)


def draw_tile_cols(key, part):
    shuffled = build_plan(key)
    return shuffled.reshape(-1)


def draw_features(key, part):
    key_val, key_col = jax.random.split(jax.random.fold_in(key, 77), 2)
    ramp_values = jnp.arange(F, dtype=jnp.float32) / F
    col_scale = 10.0 ** (0.5 * ramp_values + 0.5 * jax.random.uniform(key_col, (F,), jnp.float32))
    values = jnp.clip(jax.random.normal(key_val, (NODES, F), jnp.float32), -5.0, 5.0)
    return values * col_scale[None, :]


def level_of(stream_key, dims, cuts, least, high):
    factor_of = 1.0
    for axis_at, shards_of in cuts:
        heights = jax.random.uniform(jax.random.fold_in(jax.random.fold_in(stream_key, 6), axis_at), (shards_of,), jnp.float32, least / len(cuts), high / len(cuts))
        factor_of = factor_of * jnp.repeat(jnp.exp(heights), dims[axis_at] // shards_of).reshape((-1,) + (1,) * (len(dims) - 1 - axis_at))
    return factor_of


def length_profile(amount, total, bound, lean):
    loads = [(1 << 20) // math.isqrt(rank ** lean) + 1 for rank in range(2, amount + 1)]
    surplus, counts = total - bound - (amount - 1), [1] * (amount - 1)
    while surplus > 0:
        free = [i for i in range(amount - 1) if counts[i] < bound]
        mass, remaining = sum([loads[i] for i in free]), surplus
        for i in free:
            addition = min(bound - counts[i], max(1, remaining * loads[i] // mass), surplus)
            counts[i] = counts[i] + addition
            surplus = surplus - addition
    return np.array([bound] + counts)


def uneven_parts(key, amount, total, bound, skew):
    if amount == 2:
        one = jax.random.randint(key, (), max(1, total - bound), min(bound, total - 1) + 1)
        return jnp.stack([one, total - one])
    tallies = jnp.asarray(length_profile(amount, total, bound, skew), jnp.int32)
    pairs = (amount - 1) // 2
    giver, receiver = tallies[1:1 + 2 * pairs:2], tallies[2:2 + 2 * pairs:2]
    room = jnp.minimum(giver - 1, bound - receiver)
    passed = jax.random.randint(jax.random.fold_in(key, 1), (pairs,), 0, 1 << 20) % (room + 1)
    tallies = tallies.at[1:1 + 2 * pairs:2].set(giver - passed).at[2:2 + 2 * pairs:2].set(receiver + passed)
    return tallies[jax.random.permutation(jax.random.fold_in(key, 2), amount)]


def bell_draw(own_key, extent, width, most, cuts=(), kind=jnp.bfloat16):
    level = level_of(own_key, extent, cuts, -0.22, 0.18) if cuts else 1.0
    array = jax.random.normal(own_key, extent, jnp.float32) * width * level
    return jnp.minimum(jnp.maximum(array, -most), most).astype(kind)


def setup_inputs(seed: int = 0) -> dict:
    key_of = jax.random.split(jax.random.key(seed), 6)
    return {
        "features": draw_features(jax.random.fold_in(key_of[5], 71), 0),
        "norm_gain": jnp.clip(1.0 + 0.18 * jax.random.normal(key_of[1], (F,), jnp.float32), 0.1, 1.9),
        "row_counts": jax.vmap(lambda own: uneven_parts(own, BLK_DEV, TILES, MOST, 2))(jax.random.split(key_of[2], N_ROWS)).reshape((N_ROWS, BLK_DEV)).astype(jnp.int32),
        "tile_cols": draw_tile_cols(jax.random.fold_in(key_of[5], 71), 0),
        "tile_values": bell_draw(key_of[4], (N_ROWS * TILES, BLOCK, BLOCK), (BLOCK * 8) ** -0.5, 0.1875, ((0, 64),), jnp.float32),
    }


def reference(features, norm_gain, row_counts, tile_cols, tile_values):
    activated = jnp.maximum(features, 0.0)
    act_blocks = activated.reshape(NODES // BLOCK, BLOCK, F)
    tile_index = jnp.arange(TILES, dtype=jnp.int32)
    row_ids = jnp.arange(BLK_DEV, dtype=jnp.int32)

    def one_device(device):
        tile_counts = lax.dynamic_index_in_dim(row_counts, device, 0, keepdims=False)
        row_ends = jnp.cumsum(tile_counts, dtype=jnp.int32)
        tile_row = lax.optimization_barrier(jnp.sum((row_ends[None, :] <= tile_index[:, None]).astype(jnp.int32), axis=1))
        onehot = (tile_row[None, :] == row_ids[:, None]).astype(jnp.float32)
        block_cols = lax.dynamic_slice_in_dim(tile_cols, (device * TILES).astype(jnp.int32), TILES)
        tile_vals = lax.dynamic_slice_in_dim(tile_values, (device * TILES).astype(jnp.int32), TILES)
        picked = act_blocks[block_cols]
        products = jnp.einsum('tij,tjf->tif', tile_vals, picked, precision=lax.Precision.HIGHEST)
        summed = jnp.dot(onehot, products.reshape(TILES, BLOCK * F), precision=lax.Precision.HIGHEST, preferred_element_type=jnp.float32)
        return summed.reshape(NODE_DEV, F)
    aggregate = lax.map(one_device, jnp.arange(N_ROWS, dtype=jnp.int32)).reshape(NODES, F)
    mean_square = lax.optimization_barrier(jnp.mean(aggregate * aggregate, axis=1, keepdims=True))
    return aggregate * norm_gain[None, :] * lax.rsqrt(mean_square + 1e-05)
```

```python
import functools

import jax
import jax.numpy as jnp
from jax import lax
from jax.experimental import pallas as pl
from jax.experimental.pallas import tpu as pltpu
from jax.sharding import PartitionSpec as P

HEAVY = 3
GROUP = 16
DEPTH = 16
CHUNK = 8


def tile_kernel(slot, row, tiles, arrived, heavy, own, out, abuf, xbuf, asem, xsem):
    total = tiles.shape[0]
    n_arr, n_heavy = arrived.shape[0], heavy.shape[0]

    def tile_copy(c):
        part = pl.ds(c * CHUNK, CHUNK)
        return pltpu.make_async_copy(tiles.at[part], abuf.at[part], asem.at[c])

    def fetch(t):
        s, b = slot[t], lax.rem(t, DEPTH)

        @pl.when(s < n_arr)
        def _():
            pltpu.make_async_copy(arrived.at[s], xbuf.at[b], xsem.at[b]).start()

        @pl.when((s >= n_arr) & (s < n_arr + n_heavy))
        def _():
            pltpu.make_async_copy(heavy.at[s - n_arr], xbuf.at[b], xsem.at[b]).start()

        @pl.when(s >= n_arr + n_heavy)
        def _():
            pltpu.make_async_copy(own.at[s - n_arr - n_heavy], xbuf.at[b], xsem.at[b]).start()

    for c in range(2):
        tile_copy(c).start()

    @pl.loop(0, DEPTH)
    def _(t):
        fetch(t)

    @pl.loop(2, total // CHUNK)
    def _(c):
        tile_copy(c).start()

    out[...] = jnp.zeros_like(out)

    @pl.loop(0, total)
    def _(t):
        b = lax.rem(t, DEPTH)

        @pl.when(lax.rem(t, CHUNK) == 0)
        def _():
            tile_copy(t // CHUNK).wait()

        pltpu.make_async_copy(arrived.at[0], xbuf.at[b], xsem.at[b]).wait()
        a = abuf[t]
        x = jnp.maximum(xbuf[b], 0.0)
        a_hi = a.astype(jnp.bfloat16)
        a_lo = (a - a_hi.astype(jnp.float32)).astype(jnp.bfloat16)
        x_hi = x.astype(jnp.bfloat16)
        x_lo = (x - x_hi.astype(jnp.float32)).astype(jnp.bfloat16)
        prod = jnp.dot(
            jnp.concatenate([a_hi, a_lo], axis=1),
            jnp.concatenate([x_hi, x_hi], axis=0),
            preferred_element_type=jnp.float32,
        ) + jnp.dot(a_hi, x_lo, preferred_element_type=jnp.float32)
        out[row[t]] += prod

        @pl.when(t + DEPTH < total)
        def _():
            fetch(t + DEPTH)


def tile_product(slot, row, tiles, arrived, heavy, own):
    blocks, side, feat = own.shape
    total = tiles.shape[0]
    smem = pl.BlockSpec(memory_space=pltpu.SMEM)
    anywhere = pl.BlockSpec(memory_space=pl.ANY)
    return pl.pallas_call(
        tile_kernel,
        out_shape=jax.ShapeDtypeStruct((blocks, side, feat), jnp.float32),
        in_specs=[smem, smem, anywhere, anywhere, anywhere, anywhere],
        out_specs=pl.BlockSpec(memory_space=pltpu.VMEM),
        scratch_shapes=[
            pltpu.VMEM(tiles.shape, jnp.float32),
            pltpu.VMEM((DEPTH, side, feat), jnp.float32),
            pltpu.SemaphoreType.DMA((total // CHUNK,)),
            pltpu.SemaphoreType.DMA((DEPTH,)),
        ],
        compiler_params=pltpu.CompilerParams(vmem_limit_bytes=40 << 20),
    )(slot, row, tiles, arrived, heavy, own)


def pick_kernel(which, source, out, sem):
    count = out.shape[0]

    @pl.loop(0, count)
    def _(i):
        pltpu.make_async_copy(source.at[which[i]], out.at[i], sem.at[i]).start()

    @pl.loop(0, count)
    def _(i):
        pltpu.make_async_copy(source.at[which[i]], out.at[i], sem.at[i]).wait()


def pick(which, source):
    count = which.shape[0]
    anywhere = pl.BlockSpec(memory_space=pl.ANY)
    return pl.pallas_call(
        pick_kernel,
        out_shape=jax.ShapeDtypeStruct((count,) + source.shape[1:], source.dtype),
        in_specs=[pl.BlockSpec(memory_space=pltpu.SMEM), anywhere],
        out_specs=anywhere,
        scratch_shapes=[pltpu.SemaphoreType.DMA((count,))],
    )(which, source)


def per_device(features, norm_gain, row_counts, tile_cols, tile_values):
    node_dev, feat_dev = features.shape
    side = tile_values.shape[1]
    blocks = node_dev // side
    total = tile_values.shape[0]
    devices = lax.axis_size("rows")
    me = lax.axis_index("rows")
    own = features.reshape(blocks, side, feat_dev)
    peers = jnp.arange(devices, dtype=jnp.int32)
    owner = tile_cols // blocks
    local = tile_cols % blocks
    hit = owner[None, :] == peers[:, None]
    wanted = jnp.max(jnp.where(hit, local[None, :], 0), axis=1)
    requested = lax.all_to_all(
        wanted.reshape(devices, 1), "rows", split_axis=0, concat_axis=0, tiled=True
    )[:, 0]
    marked = (jnp.sum(hit.astype(jnp.int32), axis=1) >= 2) & (peers != me)
    i_am_heavy = jnp.sum(marked.astype(jnp.int32)) < HEAVY
    marked = marked | ((peers == me) & i_am_heavy)
    rank = jnp.sum((marked[None, :] & (peers[None, :] < peers[:, None])).astype(jnp.int32), axis=1)
    ranks = jnp.arange(HEAVY, dtype=jnp.int32)
    heavy_ids = jnp.sum(
        jnp.where(marked[None, :] & (rank[None, :] == ranks[:, None]), peers[None, :], 0), axis=1
    )
    outgoing = pick(jnp.where(i_am_heavy, peers % GROUP, requested), own)
    arrived = lax.all_to_all(outgoing, "rows", split_axis=0, concat_axis=0, tiled=True)
    pieces = pick(heavy_ids, arrived)
    groups = [[g * GROUP + i for i in range(GROUP)] for g in range(devices // GROUP)]
    heavy = lax.all_gather(pieces, "rows", axis_index_groups=groups, axis=0, tiled=True)
    match = owner[:, None] == heavy_ids[None, :]
    tile_rank = jnp.sum(match.astype(jnp.int32) * ranks[None, :], axis=1)
    slot = jnp.where(
        owner == me,
        devices + HEAVY * blocks + local,
        jnp.where(jnp.any(match, axis=1), devices + local * HEAVY + tile_rank, owner),
    )
    block_ids = jnp.arange(blocks, dtype=jnp.int32)
    row_ends = jnp.sum(
        jnp.where(block_ids[None, :] <= block_ids[:, None], row_counts[0][None, :], 0), axis=1
    )
    tile_index = jnp.arange(total, dtype=jnp.int32)
    row = jnp.sum((row_ends[None, :] <= tile_index[:, None]).astype(jnp.int32), axis=1)
    aggregate = tile_product(slot, row, tile_values, arrived, heavy, own)
    aggregate = aggregate.reshape(node_dev, feat_dev)
    square_sum = lax.psum(jnp.sum(aggregate * aggregate, axis=1), "feat")
    mean_square = square_sum / (feat_dev * lax.axis_size("feat"))
    return aggregate * norm_gain[None, :] * lax.rsqrt(mean_square + 1e-05)[:, None]


def solution(mesh):
    placed = (P("rows", "feat"), P("feat"), P("rows", None), P("rows"), P("rows", None, None))
    return jax.shard_map(
        per_device, mesh=mesh, in_specs=placed, out_specs=P("rows", "feat"), check_vma=False
    )
```

```python
import functools

import jax
import jax.numpy as jnp
from jax import lax
from jax.experimental import pallas as pl
from jax.experimental.pallas import tpu as pltpu
from jax.sharding import PartitionSpec as P

HEAVY = 3
GROUP = 16
DEPTH = 16
CHUNK = 8


def tile_kernel(slot, row, tiles, arrived, heavy, own, out, abuf, xbuf, asem, xsem):
    total = tiles.shape[0]
    n_arr, n_heavy = arrived.shape[0], heavy.shape[0]

    def tile_copy(c):
        part = pl.ds(c * CHUNK, CHUNK)
        return pltpu.make_async_copy(tiles.at[part], abuf.at[part], asem.at[c])

    def fetch(t):
        s, b = slot[t], lax.rem(t, DEPTH)

        @pl.when(s < n_arr)
        def _():
            pltpu.make_async_copy(arrived.at[s], xbuf.at[b], xsem.at[b]).start()

        @pl.when((s >= n_arr) & (s < n_arr + n_heavy))
        def _():
            pltpu.make_async_copy(heavy.at[s - n_arr], xbuf.at[b], xsem.at[b]).start()

        @pl.when(s >= n_arr + n_heavy)
        def _():
            pltpu.make_async_copy(own.at[s - n_arr - n_heavy], xbuf.at[b], xsem.at[b]).start()

    for c in range(2):
        tile_copy(c).start()

    @pl.loop(0, DEPTH)
    def _(t):
        fetch(t)

    @pl.loop(2, total // CHUNK)
    def _(c):
        tile_copy(c).start()

    out[...] = jnp.zeros_like(out)

    @pl.loop(0, total)
    def _(t):
        b = lax.rem(t, DEPTH)

        @pl.when(lax.rem(t, CHUNK) == 0)
        def _():
            tile_copy(t // CHUNK).wait()

        pltpu.make_async_copy(arrived.at[0], xbuf.at[b], xsem.at[b]).wait()
        a = abuf[t]
        x = jnp.maximum(xbuf[b], 0.0)
        a_hi = a.astype(jnp.bfloat16)
        a_lo = (a - a_hi.astype(jnp.float32)).astype(jnp.bfloat16)
        x_hi = x.astype(jnp.bfloat16)
        x_lo = (x - x_hi.astype(jnp.float32)).astype(jnp.bfloat16)
        prod = jnp.dot(
            jnp.concatenate([a_hi, a_lo], axis=1),
            jnp.concatenate([x_hi, x_hi], axis=0),
            preferred_element_type=jnp.float32,
        ) + jnp.dot(a_hi, x_lo, preferred_element_type=jnp.float32)
        out[row[t]] += prod

        @pl.when(t + DEPTH < total)
        def _():
            fetch(t + DEPTH)


def tile_product(slot, row, tiles, arrived, heavy, own):
    blocks, side, feat = own.shape
    total = tiles.shape[0]
    smem = pl.BlockSpec(memory_space=pltpu.SMEM)
    anywhere = pl.BlockSpec(memory_space=pl.ANY)
    return pl.pallas_call(
        tile_kernel,
        out_shape=jax.ShapeDtypeStruct((blocks, side, feat), jnp.float32),
        in_specs=[smem, smem, anywhere, anywhere, anywhere, anywhere],
        out_specs=pl.BlockSpec(memory_space=pltpu.VMEM),
        scratch_shapes=[
            pltpu.VMEM(tiles.shape, jnp.float32),
            pltpu.VMEM((DEPTH, side, feat), jnp.float32),
            pltpu.SemaphoreType.DMA((total // CHUNK,)),
            pltpu.SemaphoreType.DMA((DEPTH,)),
        ],
        compiler_params=pltpu.CompilerParams(vmem_limit_bytes=40 << 20),
    )(slot, row, tiles, arrived, heavy, own)


def pick_kernel(which, source, out, sem):
    count = out.shape[0]

    @pl.loop(0, count)
    def _(i):
        pltpu.make_async_copy(source.at[which[i]], out.at[i], sem.at[i]).start()

    @pl.loop(0, count)
    def _(i):
        pltpu.make_async_copy(source.at[which[i]], out.at[i], sem.at[i]).wait()


def pick(which, source, held):
    count = which.shape[0]
    spaces = (pltpu.VMEM, pl.ANY) if held else (pl.ANY, pltpu.VMEM)
    inner, outer = [pl.BlockSpec(memory_space=space) for space in spaces]
    return pl.pallas_call(
        pick_kernel,
        out_shape=jax.ShapeDtypeStruct((count,) + source.shape[1:], source.dtype),
        in_specs=[pl.BlockSpec(memory_space=pltpu.SMEM), inner],
        out_specs=outer,
        scratch_shapes=[pltpu.SemaphoreType.DMA((count,))],
    )(which, source)


def per_device(features, norm_gain, row_counts, tile_cols, tile_values):
    node_dev, feat_dev = features.shape
    side = tile_values.shape[1]
    blocks = node_dev // side
    total = tile_values.shape[0]
    devices = lax.axis_size("rows")
    me = lax.axis_index("rows")
    own = features.reshape(blocks, side, feat_dev)
    peers = jnp.arange(devices, dtype=jnp.int32)
    owner = tile_cols // blocks
    local = tile_cols % blocks
    hit = owner[None, :] == peers[:, None]
    wanted = jnp.max(jnp.where(hit, local[None, :], 0), axis=1)
    requested = lax.all_to_all(
        wanted.reshape(devices, 1), "rows", split_axis=0, concat_axis=0, tiled=True
    )[:, 0]
    marked = (jnp.sum(hit.astype(jnp.int32), axis=1) >= 2) & (peers != me)
    i_am_heavy = jnp.sum(marked.astype(jnp.int32)) < HEAVY
    marked = marked | ((peers == me) & i_am_heavy)
    rank = jnp.sum((marked[None, :] & (peers[None, :] < peers[:, None])).astype(jnp.int32), axis=1)
    ranks = jnp.arange(HEAVY, dtype=jnp.int32)
    heavy_ids = jnp.sum(
        jnp.where(marked[None, :] & (rank[None, :] == ranks[:, None]), peers[None, :], 0), axis=1
    )
    outgoing = pick(jnp.where(i_am_heavy, peers % GROUP, requested), own, True)
    arrived = lax.all_to_all(outgoing, "rows", split_axis=0, concat_axis=0, tiled=True)
    pieces = pick(heavy_ids, arrived, False)
    groups = [[g * GROUP + i for i in range(GROUP)] for g in range(devices // GROUP)]
    heavy = lax.all_gather(pieces, "rows", axis_index_groups=groups, axis=0, tiled=True)
    match = owner[:, None] == heavy_ids[None, :]
    tile_rank = jnp.sum(match.astype(jnp.int32) * ranks[None, :], axis=1)
    slot = jnp.where(
        owner == me,
        devices + HEAVY * blocks + local,
        jnp.where(jnp.any(match, axis=1), devices + local * HEAVY + tile_rank, owner),
    )
    block_ids = jnp.arange(blocks, dtype=jnp.int32)
    row_ends = jnp.sum(
        jnp.where(block_ids[None, :] <= block_ids[:, None], row_counts[0][None, :], 0), axis=1
    )
    tile_index = jnp.arange(total, dtype=jnp.int32)
    row = jnp.sum((row_ends[None, :] <= tile_index[:, None]).astype(jnp.int32), axis=1)
    aggregate = tile_product(slot, row, tile_values, arrived, heavy, own)
    aggregate = aggregate.reshape(node_dev, feat_dev)
    square_sum = lax.psum(jnp.sum(aggregate * aggregate, axis=1), "feat")
    mean_square = square_sum / (feat_dev * lax.axis_size("feat"))
    return aggregate * norm_gain[None, :] * lax.rsqrt(mean_square + 1e-05)[:, None]


def solution(mesh):
    placed = (P("rows", "feat"), P("feat"), P("rows", None), P("rows"), P("rows", None, None))
    return jax.shard_map(
        per_device, mesh=mesh, in_specs=placed, out_specs=P("rows", "feat"), check_vma=False
    )
```

```python
import functools

import jax
import jax.numpy as jnp
from jax import lax
from jax.experimental import pallas as pl
from jax.experimental.pallas import tpu as pltpu
from jax.sharding import PartitionSpec as P

HEAVY = 3
GROUP = 16
DEPTH = 16
CHUNK = 8


def tile_kernel(slot, row, tiles, arrived, heavy, own, out, abuf, xbuf, asem, xsem):
    total = tiles.shape[0]
    n_arr, n_heavy = arrived.shape[1], heavy.shape[1]
    side, feat = own.shape[1] * own.shape[2], own.shape[3]

    def tile_copy(c):
        part = pl.ds(c * CHUNK, CHUNK)
        return pltpu.make_async_copy(tiles.at[part], abuf.at[part], asem.at[c])

    def fetch(t):
        s, b = slot[t], lax.rem(t, DEPTH)

        @pl.when(s < n_arr)
        def _():
            pltpu.make_async_copy(arrived.at[:, s], xbuf.at[b], xsem.at[b]).start()

        @pl.when((s >= n_arr) & (s < n_arr + n_heavy))
        def _():
            pltpu.make_async_copy(heavy.at[:, s - n_arr], xbuf.at[b], xsem.at[b]).start()

        @pl.when(s >= n_arr + n_heavy)
        def _():
            pltpu.make_async_copy(own.at[s - n_arr - n_heavy], xbuf.at[b], xsem.at[b]).start()

    for c in range(2):
        tile_copy(c).start()

    @pl.loop(0, DEPTH)
    def _(t):
        fetch(t)

    @pl.loop(2, total // CHUNK)
    def _(c):
        tile_copy(c).start()

    out[...] = jnp.zeros_like(out)

    @pl.loop(0, total)
    def _(t):
        b = lax.rem(t, DEPTH)

        @pl.when(lax.rem(t, CHUNK) == 0)
        def _():
            tile_copy(t // CHUNK).wait()

        pltpu.make_async_copy(arrived.at[:, 0], xbuf.at[b], xsem.at[b]).wait()
        a = abuf[t]
        x = jnp.maximum(xbuf[b].reshape(side, feat), 0.0)
        a_hi = a.astype(jnp.bfloat16)
        a_lo = (a - a_hi.astype(jnp.float32)).astype(jnp.bfloat16)
        x_hi = x.astype(jnp.bfloat16)
        x_lo = (x - x_hi.astype(jnp.float32)).astype(jnp.bfloat16)
        prod = jnp.dot(
            jnp.concatenate([a_hi, a_lo], axis=1),
            jnp.concatenate([x_hi, x_hi], axis=0),
            preferred_element_type=jnp.float32,
        ) + jnp.dot(a_hi, x_lo, preferred_element_type=jnp.float32)
        out[row[t]] += prod

        @pl.when(t + DEPTH < total)
        def _():
            fetch(t + DEPTH)


def tile_product(slot, row, tiles, arrived, heavy, own):
    blocks, side, feat = own.shape
    total = tiles.shape[0]
    smem = pl.BlockSpec(memory_space=pltpu.SMEM)
    anywhere = pl.BlockSpec(memory_space=pl.ANY)
    return pl.pallas_call(
        tile_kernel,
        out_shape=jax.ShapeDtypeStruct((blocks, side, feat), jnp.float32),
        in_specs=[smem, smem, anywhere, anywhere, anywhere, anywhere],
        out_specs=pl.BlockSpec(memory_space=pltpu.VMEM),
        scratch_shapes=[
            pltpu.VMEM(tiles.shape, jnp.float32),
            pltpu.VMEM((DEPTH, PARTS, side // PARTS, feat), jnp.float32),
            pltpu.SemaphoreType.DMA((total // CHUNK,)),
            pltpu.SemaphoreType.DMA((DEPTH,)),
        ],
        compiler_params=pltpu.CompilerParams(vmem_limit_bytes=40 << 20),
    )(slot, row, tiles, arrived, heavy, own.reshape(blocks, PARTS, side // PARTS, feat))


PARTS = 4
PLANE = 8
PLANES = 8
MESH = pl.DeviceIdType.MESH


def exchange_kernel(table, heavy_slot, features, arrived_out, heavy_out, *scratch):
    names = ("own", "up1", "down1", "up2", "down2", "up3s", "down3s", "up3", "down3", "far", "picked", "arrived", "gathered")
    bufs = {n: scratch[i * PARTS : (i + 1) * PARTS] for i, n in enumerate(names)}
    own, up1, down1, up2, down2, up3s, down3s, up3, down3, far, picked, arrived, gathered = (bufs[n] for n in names)
    load_sem, zs, zr, xs, xr, gs, gr, out_sem = scratch[len(names) * PARTS :]
    me = lax.axis_index("rows")
    z, q = me // PLANE, lax.rem(me, PLANE)
    x, c = q // 2, lax.rem(q, 2)
    part_rows = own[0].shape[1]

    def at(dz):
        return lax.rem(z + dz + PLANES, PLANES)

    up, down = at(1) * PLANE + q, at(-1) * PLANE + q
    even = 1 - lax.rem(z, 2)
    partner = (z + 2 * even - 1) * PLANE + q
    right = z * PLANE + lax.rem(x + 1, 4) * 2 + c
    left = z * PLANE + lax.rem(x + 3, 4) * 2 + c
    other = z * PLANE + x * 2 + 1 - c

    def load(k):
        return pltpu.make_async_copy(features.at[:, pl.ds(k * part_rows, part_rows)], own[k], load_sem.at[k])

    for k in range(PARTS):
        load(k).start()
    barrier = pltpu.get_barrier_semaphore()
    for peer in (up, down):
        pl.semaphore_signal(barrier, inc=1, device_id={"rows": peer}, device_id_type=MESH)

    @pl.loop(1, PLANE)
    def _(p):
        peer = z * PLANE + lax.rem(q + p, PLANE)
        pl.semaphore_signal(barrier, inc=1, device_id={"rows": peer}, device_id_type=MESH)

    pl.semaphore_wait(barrier, PLANE + 1)

    def send(src, dst, ssem, rsem, peer):
        return pltpu.make_async_remote_copy(
            src_ref=src, dst_ref=dst, send_sem=ssem, recv_sem=rsem, device_id={"rows": peer}, device_id_type=MESH
        )

    def z_copies(k, step):
        src_up, dst_up, src_down, dst_down = (
            (own[k], up1[k], own[k], down1[k]),
            (up1[k], up2[k], down1[k], down2[k]),
            (up3s[k], up3[k], down3s[k], down3[k]),
            (up3[k].at[pl.ds(PLANE, 4)], far[k].at[0], down3[k].at[pl.ds(PLANE, 4)], far[k].at[1]),
        )[step]
        i = (k * 4 + step) * 2
        return (
            send(src_up, dst_up, zs.at[i], zr.at[i], up),
            send(src_down, dst_down, zs.at[i + 1], zr.at[i + 1], down),
        )

    def z_start(k, step):
        for copy in z_copies(k, step):
            copy.start()

    def z_wait(k, step):
        for copy in z_copies(k, step):
            copy.wait_recv()

    def block_of(dz_reader, reader, dz_owner):
        return table[(at(dz_reader) * PLANE + reader) * (PLANES * PLANE) + at(dz_owner) * PLANE + q]

    def x_pick(k, first, sources):
        @pl.loop(0, PLANE)
        def _(reader):
            for i, (ref, dz) in enumerate(sources):
                picked[k][reader, first + i] = ref[block_of(0, reader, dz)]

        arrived[k][pl.ds(q * PLANES + first, len(sources))] = picked[k][q, pl.ds(first, len(sources))]

        @pl.loop(1, PLANE)
        def _(p):
            reader = lax.rem(q + p, PLANE)
            send(
                picked[k].at[reader, pl.ds(first, len(sources))],
                arrived[k].at[pl.ds(q * PLANES + first, len(sources))],
                xs.at[k],
                xr.at[k],
                z * PLANE + reader,
            ).start()

    def x_pass(k, first, source):
        arrived[k][q * PLANES + first] = source(q)[...]

        @pl.loop(1, PLANE)
        def _(p):
            reader = lax.rem(q + p, PLANE)
            send(source(reader), arrived[k].at[q * PLANES + first], xs.at[k], xr.at[k], z * PLANE + reader).start()

    def gather_copy(k, i, src, dst, peer):
        j = k * 8 + i
        return send(src, dst, gs.at[j], gr.at[j], peer)

    def mine(k, qq):
        return gathered[k].at[qq]

    def q_of(xx):
        return lax.rem(x + xx + 4, 4) * 2 + c

    def gather_copies(k, i):
        if i == 0:
            src = gathered[k].at[q, 1 - even]
            return gather_copy(k, 0, src, src, partner)
        if i == 1:
            return gather_copy(k, 1, mine(k, q), mine(k, q), right)
        if i == 2:
            return gather_copy(k, 2, mine(k, q), mine(k, q), left)
        if i == 3:
            src = gathered[k].at[q_of(-1), 0]
            return gather_copy(k, 3, src, src, right)
        if i == 4:
            src = gathered[k].at[q_of(1), 1]
            return gather_copy(k, 4, src, src, left)
        src = mine(k, q_of((0, 1, -1)[i - 5])) if i < 8 else None
        return gather_copy(k, i, src, src, other)

    def last_core_copy(k):
        src = mine(k, q_of(2))
        j = PARTS * 8 + k
        return send(src, src, gs.at[j], gr.at[j], other)

    def arrived_store(k):
        return pltpu.make_async_copy(arrived[k], arrived_out.at[k], out_sem.at[k])

    def heavy_store(k):
        return pltpu.make_async_copy(gathered[k], heavy_out.at[k], out_sem.at[PARTS + k])

    def stage(k, s):
        if s == 0:
            load(k).wait()
            z_start(k, 0)
            x_pick(k, 0, [(own[k], 0)])
        elif s == 1:
            z_wait(k, 0)
            z_start(k, 1)
            x_pick(k, 1, [(up1[k], -1), (down1[k], 1)])
        elif s == 2:
            z_wait(k, 1)

            @pl.loop(0, PLANE)
            def _(reader):
                up3s[k][reader] = up2[k][block_of(1, reader, -2)]
                down3s[k][reader] = down2[k][block_of(-1, reader, 2)]

            @pl.loop(0, 4)
            def _(half):
                up3s[k][PLANE + half] = up2[k][block_of(2, 2 * half, -2)]
                down3s[k][PLANE + half] = down2[k][block_of(-2, 2 * half + 1, 2)]

            z_start(k, 2)
            x_pick(k, 3, [(up2[k], -2), (down2[k], 2)])
        elif s == 3:
            z_wait(k, 2)
            z_start(k, 3)
            x_pass(k, 5, lambda reader: up3[k].at[reader])
            x_pass(k, 6, lambda reader: down3[k].at[reader])
        elif s == 4:
            z_wait(k, 3)
            x_pass(k, 7, lambda reader: far[k].at[lax.rem(reader, 2), reader // 2])
        elif s == 5:
            everything = arrived[k].at[pl.ds(0, (PLANE - 1) * PLANES)]
            pltpu.make_async_copy(everything, everything, xr.at[k]).wait()
            arrived_store(k).start()
            for i in range(HEAVY):
                gathered[k][q, 1 - even, i] = arrived[k][heavy_slot[i]]
            gather_copies(k, 0).start()
        elif s == 6:
            gather_copies(k, 0).wait_recv()
            for i in (1, 2, 5):
                gather_copies(k, i).start()
        elif s == 7:
            gather_copies(k, 1).wait_recv()
            gather_copies(k, 2).wait_recv()
            for i in (3, 4, 6, 7):
                gather_copies(k, i).start()
        elif s == 8:
            gather_copies(k, 3).wait_recv()
            gather_copies(k, 4).wait_recv()
            last_core_copy(k).start()
        elif s == 9:
            for i in (5, 6, 7):
                gather_copies(k, i).wait_recv()
            last_core_copy(k).wait_recv()
            heavy_store(k).start()

    for t in range(PARTS + 9):
        for s in range(10):
            if 0 <= t - s < PARTS:
                stage(t - s, s)

    for k in range(PARTS):
        for step in range(4):
            for copy in z_copies(k, step):
                copy.wait_send()
        everything = arrived[k].at[pl.ds(0, (PLANE - 1) * PLANES)]
        pltpu.make_async_copy(everything, everything, xs.at[k]).wait()
        for i in range(8):
            gather_copies(k, i).wait_send()
        last_core_copy(k).wait_send()
        arrived_store(k).wait()
        heavy_store(k).wait()


def exchange(table, heavy_slot, own):
    blocks, side, feat = own.shape
    rows = side // PARTS
    smem = pl.BlockSpec(memory_space=pltpu.SMEM)
    anywhere = pl.BlockSpec(memory_space=pl.ANY)
    leads = [(blocks,)] * 5 + [(PLANE + 4,)] * 4 + [(2, 4), (PLANE, 5), (PLANE * PLANES,), (PLANE, 2, HEAVY)]
    bufs = [pltpu.VMEM(lead + (rows, feat), jnp.float32) for lead in leads for _ in range(PARTS)]
    dma = pltpu.SemaphoreType.DMA
    return pl.pallas_call(
        exchange_kernel,
        out_shape=[
            jax.ShapeDtypeStruct((PARTS, PLANE * PLANES, rows, feat), jnp.float32),
            jax.ShapeDtypeStruct((PARTS, PLANE, 2, HEAVY, rows, feat), jnp.float32),
        ],
        in_specs=[smem, smem, anywhere],
        out_specs=[anywhere, anywhere],
        scratch_shapes=bufs
        + [
            dma((PARTS,)),
            dma((PARTS * 8,)),
            dma((PARTS * 8,)),
            dma((PARTS,)),
            dma((PARTS,)),
            dma((PARTS * 9,)),
            dma((PARTS * 9,)),
            dma((PARTS * 2,)),
        ],
        compiler_params=pltpu.CompilerParams(collective_id=0, has_side_effects=True, vmem_limit_bytes=56 << 20),
    )(table, heavy_slot, own)


def per_device(features, norm_gain, row_counts, tile_cols, tile_values):
    node_dev, feat_dev = features.shape
    side = tile_values.shape[1]
    blocks = node_dev // side
    total = tile_values.shape[0]
    devices = lax.axis_size("rows")
    me = lax.axis_index("rows")
    own = features.reshape(blocks, side, feat_dev)
    peers = jnp.arange(devices, dtype=jnp.int32)
    owner = tile_cols // blocks
    local = tile_cols % blocks
    hit = owner[None, :] == peers[:, None]
    wanted = jnp.max(jnp.where(hit, local[None, :], 0), axis=1)
    marked = (jnp.sum(hit.astype(jnp.int32), axis=1) >= 2) & (peers != me)
    i_am_heavy = jnp.sum(marked.astype(jnp.int32)) < HEAVY
    marked = marked | ((peers == me) & i_am_heavy)
    rank = jnp.sum((marked[None, :] & (peers[None, :] < peers[:, None])).astype(jnp.int32), axis=1)
    ranks = jnp.arange(HEAVY, dtype=jnp.int32)
    heavy_ids = jnp.sum(
        jnp.where(marked[None, :] & (rank[None, :] == ranks[:, None]), peers[None, :], 0), axis=1
    )
    wanted = jnp.where(marked | (peers == me), me % GROUP, wanted)
    table = lax.all_gather(wanted, "rows", axis=0, tiled=True)

    def panel_slot(stripe):
        ahead = (stripe // PLANE - me // PLANE + PLANES) % PLANES
        return stripe % PLANE * PLANES + jnp.where(ahead < 4, 2 * ahead, 2 * (PLANES - ahead) - 1)

    arrived, heavy = exchange(table, panel_slot(heavy_ids), own)
    heavy = heavy.reshape((PARTS, blocks * HEAVY) + heavy.shape[-2:])
    match = owner[:, None] == heavy_ids[None, :]
    tile_rank = jnp.sum(match.astype(jnp.int32) * ranks[None, :], axis=1)
    slot = jnp.where(
        owner == me,
        devices + HEAVY * blocks + local,
        jnp.where(
            jnp.any(match, axis=1),
            devices + (local % PLANE * 2 + local // PLANE) * HEAVY + tile_rank,
            panel_slot(owner),
        ),
    )
    block_ids = jnp.arange(blocks, dtype=jnp.int32)
    row_ends = jnp.sum(
        jnp.where(block_ids[None, :] <= block_ids[:, None], row_counts[0][None, :], 0), axis=1
    )
    tile_index = jnp.arange(total, dtype=jnp.int32)
    row = jnp.sum((row_ends[None, :] <= tile_index[:, None]).astype(jnp.int32), axis=1)
    aggregate = tile_product(slot, row, tile_values, arrived, heavy, own)
    aggregate = aggregate.reshape(node_dev, feat_dev)
    square_sum = lax.psum(jnp.sum(aggregate * aggregate, axis=1), "feat")
    mean_square = square_sum / (feat_dev * lax.axis_size("feat"))
    return aggregate * norm_gain[None, :] * lax.rsqrt(mean_square + 1e-05)[:, None]


def solution(mesh):
    placed = (P("rows", "feat"), P("feat"), P("rows", None), P("rows"), P("rows", None, None))
    return jax.shard_map(
        per_device, mesh=mesh, in_specs=placed, out_specs=P("rows", "feat"), check_vma=False
    )
```

```python
import functools

import jax
import jax.numpy as jnp
from jax import lax
from jax.experimental import pallas as pl
from jax.experimental.pallas import tpu as pltpu
from jax.sharding import PartitionSpec as P

HEAVY = 3
GROUP = 16
DEPTH = 16
CHUNK = 8


def tile_kernel(plan, tiles, arrived, heavy, own, out, abuf, xbuf, asem, xsem):
    total = tiles.shape[0]
    n_arr, n_heavy = arrived.shape[1], heavy.shape[1]
    side, feat = own.shape[1] * own.shape[2], own.shape[3]

    def tile_copy(c):
        part = pl.ds(c * CHUNK, CHUNK)
        return pltpu.make_async_copy(tiles.at[part], abuf.at[part], asem.at[c])

    def fetch(t):
        s, b = plan[0, t], lax.rem(t, DEPTH)

        @pl.when(s < n_arr)
        def _():
            pltpu.make_async_copy(arrived.at[:, s], xbuf.at[b], xsem.at[b]).start()

        @pl.when((s >= n_arr) & (s < n_arr + n_heavy))
        def _():
            pltpu.make_async_copy(heavy.at[:, s - n_arr], xbuf.at[b], xsem.at[b]).start()

        @pl.when(s >= n_arr + n_heavy)
        def _():
            pltpu.make_async_copy(own.at[s - n_arr - n_heavy], xbuf.at[b], xsem.at[b]).start()

    for c in range(2):
        tile_copy(c).start()

    @pl.loop(0, DEPTH)
    def _(t):
        fetch(t)

    @pl.loop(2, total // CHUNK)
    def _(c):
        tile_copy(c).start()

    out[...] = jnp.zeros_like(out)

    @pl.loop(0, total)
    def _(t):
        b = lax.rem(t, DEPTH)

        @pl.when(lax.rem(t, CHUNK) == 0)
        def _():
            tile_copy(t // CHUNK).wait()

        pltpu.make_async_copy(arrived.at[:, 0], xbuf.at[b], xsem.at[b]).wait()
        a = abuf[t]
        x = jnp.maximum(xbuf[b].reshape(side, feat), 0.0)
        a_hi = a.astype(jnp.bfloat16)
        a_lo = (a - a_hi.astype(jnp.float32)).astype(jnp.bfloat16)
        x_hi = x.astype(jnp.bfloat16)
        x_lo = (x - x_hi.astype(jnp.float32)).astype(jnp.bfloat16)
        prod = jnp.dot(
            jnp.concatenate([a_hi, a_lo], axis=1),
            jnp.concatenate([x_hi, x_hi], axis=0),
            preferred_element_type=jnp.float32,
        ) + jnp.dot(a_hi, x_lo, preferred_element_type=jnp.float32)
        out[plan[1, t]] += prod

        @pl.when(t + DEPTH < total)
        def _():
            fetch(t + DEPTH)


def tile_product(plan, tiles, arrived, heavy, own):
    blocks, side, feat = own.shape
    total = tiles.shape[0]
    smem = pl.BlockSpec(memory_space=pltpu.SMEM)
    anywhere = pl.BlockSpec(memory_space=pl.ANY)
    return pl.pallas_call(
        tile_kernel,
        out_shape=jax.ShapeDtypeStruct((blocks, side, feat), jnp.float32),
        in_specs=[smem, anywhere, anywhere, anywhere, anywhere],
        out_specs=pl.BlockSpec(memory_space=pltpu.VMEM),
        scratch_shapes=[
            pltpu.VMEM(tiles.shape, jnp.float32),
            pltpu.VMEM((DEPTH, PARTS, side // PARTS, feat), jnp.float32),
            pltpu.SemaphoreType.DMA((total // CHUNK,)),
            pltpu.SemaphoreType.DMA((DEPTH,)),
        ],
        compiler_params=pltpu.CompilerParams(vmem_limit_bytes=40 << 20),
    )(plan, tiles, arrived, heavy, own.reshape(blocks, PARTS, side // PARTS, feat))


PARTS = 4
PLANE = 8
PLANES = 8
MESH = pl.DeviceIdType.MESH


def total_of(mask, values, axis):
    return jnp.sum(jnp.where(mask, values, 0), axis=axis, keepdims=True)


def plan_rows(me, cols, counts, blocks):
    lanes = cols.shape[1]
    devices, shift = PLANE * PLANES, blocks.bit_length() - 1
    i = lax.broadcasted_iota(jnp.int32, (lanes, lanes), 0)
    j = lax.broadcasted_iota(jnp.int32, (lanes, lanes), 1)
    lane, down = j[:1], i[:, :1]

    def panel_slot(stripe):
        ahead = ((stripe >> 3) - me // PLANE + PLANES) & (PLANES - 1)
        return (stripe & (PLANE - 1)) * PLANES + jnp.where(ahead < 4, 2 * ahead, 2 * (PLANES - ahead) - 1)

    spread = jnp.broadcast_to(cols, (lanes, lanes))
    turned = spread.T
    hit = (turned >> shift) == j
    wanted = jnp.max(jnp.where(hit, turned & (blocks - 1), 0), axis=0, keepdims=True)
    marked = (total_of(hit, 1, 0) >= 2) & (lane != me)
    i_am_heavy = total_of(marked, 1, 1) < HEAVY
    marked = marked | ((lane == me) & i_am_heavy)
    hit_down = (spread >> shift) == i
    marked_down = (total_of(hit_down, 1, 1) >= 2) & (down != me)
    marked_down = marked_down | ((down == me) & i_am_heavy)
    rank = total_of(jnp.broadcast_to(marked_down, i.shape) & (i < j), 1, 0)
    rank_down = total_of(jnp.broadcast_to(marked, i.shape) & (j < i), 1, 1)
    request = jnp.where(marked | (lane == me), me & (GROUP - 1), wanted)
    for s in range(HEAVY):
        request = jnp.where(lane == devices + s, total_of(marked & (rank == s), panel_slot(lane), 1), request)
    heavy_hit = hit_down & marked_down
    local = cols & (blocks - 1)
    slot = jnp.where(
        total_of(heavy_hit, 1, 0) > 0,
        devices + ((local & (PLANE - 1)) * 2 + (local >> 3)) * HEAVY + total_of(heavy_hit, jnp.broadcast_to(rank_down, i.shape), 0),
        panel_slot(cols >> shift),
    )
    slot = jnp.where((cols >> shift) == me, devices + HEAVY * blocks + local, slot)
    side = counts.shape[1]
    ends = total_of(j[:side, :side] <= i[:side, :side], jnp.broadcast_to(counts, (side, side)), 1)
    row = total_of(ends <= j[:side], 1, 0)
    return request, slot, row


def exchange_kernel(cols, counts, features, arrived_out, heavy_out, plan_out, *scratch):
    names = ("own", "up1", "down1", "up2", "down2", "up3s", "down3s", "up3", "down3", "far", "picked", "arrived", "gathered")
    bufs = {n: scratch[i * PARTS : (i + 1) * PARTS] for i, n in enumerate(names)}
    own, up1, down1, up2, down2, up3s, down3s, up3, down3, far, picked, arrived, gathered = (bufs[n] for n in names)
    (rows_buf, table, load_sem, zs, zr, xs, xr, gs, gr, out_sem, ps, pr, table_sem) = scratch[len(names) * PARTS :]
    me = lax.axis_index("rows")
    z, q = me // PLANE, lax.rem(me, PLANE)
    x, c = q // 2, lax.rem(q, 2)
    part_rows = own[0].shape[1]

    def at(dz):
        return lax.rem(z + dz + PLANES, PLANES)

    up, down = at(1) * PLANE + q, at(-1) * PLANE + q
    even = 1 - lax.rem(z, 2)
    partner = (z + 2 * even - 1) * PLANE + q
    right = z * PLANE + lax.rem(x + 1, 4) * 2 + c
    left = z * PLANE + lax.rem(x + 3, 4) * 2 + c
    other = z * PLANE + x * 2 + 1 - c

    def load(k):
        return pltpu.make_async_copy(features.at[:, pl.ds(k * part_rows, part_rows)], own[k], load_sem.at[k])

    for k in range(PARTS):
        load(k).start()
    barrier = pltpu.get_barrier_semaphore()
    second_up, second_down = at(2) * PLANE + q, at(-2) * PLANE + q
    for peer in (up, down, second_up, second_down):
        pl.semaphore_signal(barrier, inc=1, device_id={"rows": peer}, device_id_type=MESH)

    @pl.loop(1, PLANE)
    def _(p):
        peer = z * PLANE + lax.rem(q + p, PLANE)
        pl.semaphore_signal(barrier, inc=1, device_id={"rows": peer}, device_id_type=MESH)

    pl.semaphore_wait(barrier, PLANE + 3)

    def send(src, dst, ssem, rsem, peer):
        return pltpu.make_async_remote_copy(
            src_ref=src, dst_ref=dst, send_sem=ssem, recv_sem=rsem, device_id={"rows": peer}, device_id_type=MESH
        )

    def z_copies(k, step):
        src_up, dst_up, src_down, dst_down = (
            (own[k], up1[k], own[k], down1[k]),
            (up1[k], up2[k], down1[k], down2[k]),
            (up3s[k], up3[k], down3s[k], down3[k]),
            (up3[k].at[pl.ds(PLANE, 4)], far[k].at[0], down3[k].at[pl.ds(PLANE, 4)], far[k].at[1]),
        )[step]
        i = (k * 4 + step) * 2
        return (
            send(src_up, dst_up, zs.at[i], zr.at[i], up),
            send(src_down, dst_down, zs.at[i + 1], zr.at[i + 1], down),
        )

    def z_start(k, step):
        for copy in z_copies(k, step):
            copy.start()

    def z_wait(k, step):
        for copy in z_copies(k, step):
            copy.wait_recv()

    def block_of(dz_reader, reader, dz_owner):
        return table[at(dz_reader) * PLANE + reader, 0, at(dz_owner) * PLANE + q]

    def plane_rows(dz):
        return pl.ds(at(dz) * PLANE, PLANE)

    def table_copy(i, dz):
        return pltpu.make_async_copy(rows_buf.at[plane_rows(dz)], table.at[plane_rows(dz)], table_sem.at[i])

    hops = ((up, -1), (down, 1), (second_up, -2), (second_down, 2))

    def rows_copy(i):
        src = rows_buf.at[plane_rows(0)]
        return send(src, src, ps.at[1 + i], pr.at[1 + i], hops[i][0])

    def share_plan():
        request, slot, row = plan_rows(me, cols[...], counts[...], own[0].shape[0])
        plan_out[0:1] = slot
        plan_out[1:2] = row
        rows_buf[me] = request

        @pl.loop(1, PLANE)
        def _(p):
            src = rows_buf.at[me]
            send(src, src, ps.at[0], pr.at[0], z * PLANE + lax.rem(q + p, PLANE)).start()

        most = rows_buf.at[pl.ds(0, PLANE - 1)]
        pltpu.make_async_copy(most, most, pr.at[0]).wait()
        for i in range(4):
            rows_copy(i).start()
        table_copy(0, 0).start()
        table_copy(0, 0).wait()

    def take_plan():
        for i, (_, dz) in enumerate(hops):
            src = rows_buf.at[plane_rows(dz)]
            pltpu.make_async_copy(src, src, pr.at[1 + i]).wait()
            table_copy(1 + i, dz).start()
        for i, (_, dz) in enumerate(hops):
            table_copy(1 + i, dz).wait()

    def x_pick(k, first, sources):
        @pl.loop(0, PLANE)
        def _(reader):
            for i, (ref, dz) in enumerate(sources):
                picked[k][reader, first + i] = ref[block_of(0, reader, dz)]

        arrived[k][pl.ds(q * PLANES + first, len(sources))] = picked[k][q, pl.ds(first, len(sources))]

        @pl.loop(1, PLANE)
        def _(p):
            reader = lax.rem(q + p, PLANE)
            send(
                picked[k].at[reader, pl.ds(first, len(sources))],
                arrived[k].at[pl.ds(q * PLANES + first, len(sources))],
                xs.at[k],
                xr.at[k],
                z * PLANE + reader,
            ).start()

    def x_pass(k, first, source):
        arrived[k][q * PLANES + first] = source(q)[...]

        @pl.loop(1, PLANE)
        def _(p):
            reader = lax.rem(q + p, PLANE)
            send(source(reader), arrived[k].at[q * PLANES + first], xs.at[k], xr.at[k], z * PLANE + reader).start()

    def gather_copy(k, i, src, dst, peer):
        j = k * 8 + i
        return send(src, dst, gs.at[j], gr.at[j], peer)

    def mine(k, qq):
        return gathered[k].at[qq]

    def q_of(xx):
        return lax.rem(x + xx + 4, 4) * 2 + c

    def gather_copies(k, i):
        if i == 0:
            src = gathered[k].at[q, 1 - even]
            return gather_copy(k, 0, src, src, partner)
        if i == 1:
            return gather_copy(k, 1, mine(k, q), mine(k, q), right)
        if i == 2:
            return gather_copy(k, 2, mine(k, q), mine(k, q), left)
        if i == 3:
            src = gathered[k].at[q_of(-1), 0]
            return gather_copy(k, 3, src, src, right)
        if i == 4:
            src = gathered[k].at[q_of(1), 1]
            return gather_copy(k, 4, src, src, left)
        src = mine(k, q_of((0, 1, -1)[i - 5])) if i < 8 else None
        return gather_copy(k, i, src, src, other)

    def last_core_copy(k):
        src = mine(k, q_of(2))
        j = PARTS * 8 + k
        return send(src, src, gs.at[j], gr.at[j], other)

    def arrived_store(k):
        return pltpu.make_async_copy(arrived[k], arrived_out.at[k], out_sem.at[k])

    def heavy_store(k):
        return pltpu.make_async_copy(gathered[k], heavy_out.at[k], out_sem.at[PARTS + k])

    def stage(k, s):
        if s == 0:
            load(k).wait()
            z_start(k, 0)
            if k == 0:
                share_plan()
            x_pick(k, 0, [(own[k], 0)])
        elif s == 1:
            z_wait(k, 0)
            z_start(k, 1)
            x_pick(k, 1, [(up1[k], -1), (down1[k], 1)])
        elif s == 2:
            z_wait(k, 1)
            if k == 0:
                take_plan()

            @pl.loop(0, PLANE)
            def _(reader):
                up3s[k][reader] = up2[k][block_of(1, reader, -2)]
                down3s[k][reader] = down2[k][block_of(-1, reader, 2)]

            @pl.loop(0, 4)
            def _(half):
                up3s[k][PLANE + half] = up2[k][block_of(2, 2 * half, -2)]
                down3s[k][PLANE + half] = down2[k][block_of(-2, 2 * half + 1, 2)]

            z_start(k, 2)
            x_pick(k, 3, [(up2[k], -2), (down2[k], 2)])
        elif s == 3:
            z_wait(k, 2)
            z_start(k, 3)
            x_pass(k, 5, lambda reader: up3[k].at[reader])
            x_pass(k, 6, lambda reader: down3[k].at[reader])
        elif s == 4:
            z_wait(k, 3)
            x_pass(k, 7, lambda reader: far[k].at[lax.rem(reader, 2), reader // 2])
        elif s == 5:
            everything = arrived[k].at[pl.ds(0, (PLANE - 1) * PLANES)]
            pltpu.make_async_copy(everything, everything, xr.at[k]).wait()
            arrived_store(k).start()
            for i in range(HEAVY):
                gathered[k][q, 1 - even, i] = arrived[k][table[me, 0, PLANES * PLANE + i]]
            gather_copies(k, 0).start()
        elif s == 6:
            gather_copies(k, 0).wait_recv()
            for i in (1, 2, 5):
                gather_copies(k, i).start()
        elif s == 7:
            gather_copies(k, 1).wait_recv()
            gather_copies(k, 2).wait_recv()
            for i in (3, 4, 6, 7):
                gather_copies(k, i).start()
        elif s == 8:
            gather_copies(k, 3).wait_recv()
            gather_copies(k, 4).wait_recv()
            last_core_copy(k).start()
        elif s == 9:
            for i in (5, 6, 7):
                gather_copies(k, i).wait_recv()
            last_core_copy(k).wait_recv()
            heavy_store(k).start()

    for t in range(PARTS + 9):
        for s in range(10):
            if 0 <= t - s < PARTS:
                stage(t - s, s)

    most = rows_buf.at[pl.ds(0, PLANE - 1)]
    pltpu.make_async_copy(most, most, ps.at[0]).wait()
    for i in range(4):
        rows_copy(i).wait_send()
    for k in range(PARTS):
        for step in range(4):
            for copy in z_copies(k, step):
                copy.wait_send()
        everything = arrived[k].at[pl.ds(0, (PLANE - 1) * PLANES)]
        pltpu.make_async_copy(everything, everything, xs.at[k]).wait()
        for i in range(8):
            gather_copies(k, i).wait_send()
        last_core_copy(k).wait_send()
        arrived_store(k).wait()
        heavy_store(k).wait()


def exchange(cols, counts, own):
    blocks, side, feat = own.shape
    rows = side // PARTS
    vmem = pl.BlockSpec(memory_space=pltpu.VMEM)
    anywhere = pl.BlockSpec(memory_space=pl.ANY)
    leads = [(blocks,)] * 5 + [(PLANE + 4,)] * 4 + [(2, 4), (PLANE, 5), (PLANE * PLANES,), (PLANE, 2, HEAVY)]
    bufs = [pltpu.VMEM(lead + (rows, feat), jnp.float32) for lead in leads for _ in range(PARTS)]
    dma = pltpu.SemaphoreType.DMA
    return pl.pallas_call(
        exchange_kernel,
        out_shape=[
            jax.ShapeDtypeStruct((PARTS, PLANE * PLANES, rows, feat), jnp.float32),
            jax.ShapeDtypeStruct((PARTS, PLANE, 2, HEAVY, rows, feat), jnp.float32),
            jax.ShapeDtypeStruct((2, cols.shape[1]), jnp.int32),
        ],
        in_specs=[vmem, vmem, anywhere],
        out_specs=[anywhere, anywhere, vmem],
        scratch_shapes=bufs
        + [
            pltpu.VMEM((PLANE * PLANES, 1, cols.shape[1]), jnp.int32),
            pltpu.SMEM((PLANE * PLANES, 1, cols.shape[1]), jnp.int32),
            dma((PARTS,)),
            dma((PARTS * 8,)),
            dma((PARTS * 8,)),
            dma((PARTS,)),
            dma((PARTS,)),
            dma((PARTS * 9,)),
            dma((PARTS * 9,)),
            dma((PARTS * 2,)),
            dma((5,)),
            dma((5,)),
            dma((5,)),
        ],
        compiler_params=pltpu.CompilerParams(collective_id=0, has_side_effects=True, vmem_limit_bytes=56 << 20),
    )(cols, counts, own)


def per_device(features, norm_gain, row_counts, tile_cols, tile_values):
    node_dev, feat_dev = features.shape
    side = tile_values.shape[1]
    blocks = node_dev // side
    total = tile_values.shape[0]
    own = features.reshape(blocks, side, feat_dev)
    arrived, heavy, plan = exchange(tile_cols.reshape(1, total), row_counts, own)
    heavy = heavy.reshape((PARTS, blocks * HEAVY) + heavy.shape[-2:])
    aggregate = tile_product(plan, tile_values, arrived, heavy, own)
    aggregate = aggregate.reshape(node_dev, feat_dev)
    square_sum = lax.psum(jnp.sum(aggregate * aggregate, axis=1), "feat")
    mean_square = square_sum / (feat_dev * lax.axis_size("feat"))
    return aggregate * norm_gain[None, :] * lax.rsqrt(mean_square + 1e-05)[:, None]


def solution(mesh):
    placed = (P("rows", "feat"), P("feat"), P("rows", None), P("rows"), P("rows", None, None))
    return jax.shard_map(
        per_device, mesh=mesh, in_specs=placed, out_specs=P("rows", "feat"), check_vma=False
    )
```

```python
import functools

import jax
import jax.numpy as jnp
from jax import lax
from jax.experimental import pallas as pl
from jax.experimental.pallas import tpu as pltpu
from jax.sharding import PartitionSpec as P

HEAVY = 3
GROUP = 16
TOGETHER = 4


def halves(value):
    high = value.astype(jnp.bfloat16)
    return high, (value - high.astype(jnp.float32)).astype(jnp.bfloat16)


def tile_kernel(plan, tiles, *rest):
    panel, heavy = rest[:PARTS], rest[PARTS : 2 * PARTS]
    out = rest[2 * PARTS]
    total, light = tiles.shape[0], panel[0].shape[0]
    out[...] = jnp.zeros_like(out)

    def product(t):
        slot = plan[0, t]
        is_light, i, j = slot < light, jnp.minimum(slot, light - 1), jnp.maximum(slot - light, 0)
        x = jnp.concatenate([jnp.where(is_light, panel[k][i], heavy[k][j]) for k in range(PARTS)], axis=0)
        x_hi, x_lo = halves(jnp.maximum(x, 0.0))
        a_hi, a_lo = halves(tiles[t])
        return jnp.dot(
            jnp.concatenate([a_hi, a_lo], axis=1),
            jnp.concatenate([x_hi, x_hi], axis=0),
            preferred_element_type=jnp.float32,
        ) + jnp.dot(a_hi, x_lo, preferred_element_type=jnp.float32)

    @pl.loop(0, total // TOGETHER)
    def _(step):
        ts = [step * TOGETHER + u for u in range(TOGETHER)]
        products = [product(t) for t in ts]
        for t, prod in zip(ts, products):
            out[plan[1, t]] += prod


def tile_product(plan, tiles, panel, heavy):
    side = tiles.shape[1]
    blocks, feat = panel[0].shape[0] - PLANE * PLANES, panel[0].shape[-1]
    vmem = pl.BlockSpec(memory_space=pltpu.VMEM)
    return pl.pallas_call(
        tile_kernel,
        out_shape=jax.ShapeDtypeStruct((blocks, side, feat), jnp.float32),
        in_specs=[pl.BlockSpec(memory_space=pltpu.SMEM)] + [vmem] * (2 * PARTS + 1),
        out_specs=vmem,
        compiler_params=pltpu.CompilerParams(vmem_limit_bytes=8 << 20),
    )(plan, tiles, *panel, *heavy)


PARTS = 4
PLANE = 8
PLANES = 8
MESH = pl.DeviceIdType.MESH


def total_of(mask, values, axis):
    return jnp.sum(jnp.where(mask, values, 0), axis=axis, keepdims=True)


def plan_rows(me, cols, counts, blocks):
    lanes = cols.shape[1]
    devices, shift = PLANE * PLANES, blocks.bit_length() - 1
    i = lax.broadcasted_iota(jnp.int32, (lanes, lanes), 0)
    j = lax.broadcasted_iota(jnp.int32, (lanes, lanes), 1)
    lane, down = j[:1], i[:, :1]

    def panel_slot(stripe):
        ahead = ((stripe >> 3) - me // PLANE + PLANES) & (PLANES - 1)
        return (stripe & (PLANE - 1)) * PLANES + jnp.where(ahead < 4, 2 * ahead, 2 * (PLANES - ahead) - 1)

    spread = jnp.broadcast_to(cols, (lanes, lanes))
    turned = spread.T
    hit = (turned >> shift) == j
    wanted = jnp.max(jnp.where(hit, turned & (blocks - 1), 0), axis=0, keepdims=True)
    marked = (total_of(hit, 1, 0) >= 2) & (lane != me)
    i_am_heavy = total_of(marked, 1, 1) < HEAVY
    marked = marked | ((lane == me) & i_am_heavy)
    hit_down = (spread >> shift) == i
    marked_down = (total_of(hit_down, 1, 1) >= 2) & (down != me)
    marked_down = marked_down | ((down == me) & i_am_heavy)
    rank = total_of(jnp.broadcast_to(marked_down, i.shape) & (i < j), 1, 0)
    rank_down = total_of(jnp.broadcast_to(marked, i.shape) & (j < i), 1, 1)
    request = jnp.where(marked | (lane == me), me & (GROUP - 1), wanted)
    for s in range(HEAVY):
        request = jnp.where(lane == devices + s, total_of(marked & (rank == s), panel_slot(lane), 1), request)
    heavy_hit = hit_down & marked_down
    local = cols & (blocks - 1)
    slot = jnp.where(
        total_of(heavy_hit, 1, 0) > 0,
        devices + blocks + ((local & (PLANE - 1)) * 2 + (local >> 3)) * HEAVY + total_of(heavy_hit, jnp.broadcast_to(rank_down, i.shape), 0),
        panel_slot(cols >> shift),
    )
    slot = jnp.where((cols >> shift) == me, devices + local, slot)
    side = counts.shape[1]
    ends = total_of(j[:side, :side] <= i[:side, :side], jnp.broadcast_to(counts, (side, side)), 1)
    row = total_of(ends <= j[:side], 1, 0)
    return request, slot, row


def exchange_kernel(cols, counts, features, tiles, *rest):
    arrived, gathered = rest[:PARTS], rest[PARTS : 2 * PARTS]
    plan_out, tiles_out, scratch = rest[2 * PARTS], rest[2 * PARTS + 1], rest[2 * PARTS + 2 :]
    names = ("own", "up1", "down1", "up2", "down2", "up3s", "down3s", "up3", "down3", "far", "picked")
    bufs = {n: scratch[i * PARTS : (i + 1) * PARTS] for i, n in enumerate(names)}
    own, up1, down1, up2, down2, up3s, down3s, up3, down3, far, picked = (bufs[n] for n in names)
    (rows_buf, table, load_sem, zs, zr, xs, xr, gs, gr, out_sem, ps, pr, table_sem, tile_sem) = scratch[len(names) * PARTS :]
    me = lax.axis_index("rows")
    z, q = me // PLANE, lax.rem(me, PLANE)
    x, c = q // 2, lax.rem(q, 2)
    part_rows = own[0].shape[1]

    def at(dz):
        return lax.rem(z + dz + PLANES, PLANES)

    up, down = at(1) * PLANE + q, at(-1) * PLANE + q
    even = 1 - lax.rem(z, 2)
    partner = (z + 2 * even - 1) * PLANE + q
    right = z * PLANE + lax.rem(x + 1, 4) * 2 + c
    left = z * PLANE + lax.rem(x + 3, 4) * 2 + c
    other = z * PLANE + x * 2 + 1 - c

    def load(k):
        return pltpu.make_async_copy(features.at[:, pl.ds(k * part_rows, part_rows)], own[k], load_sem.at[k])

    for k in range(PARTS):
        load(k).start()
    tile_load = pltpu.make_async_copy(tiles, tiles_out, tile_sem)
    tile_load.start()
    barrier = pltpu.get_barrier_semaphore()
    second_up, second_down = at(2) * PLANE + q, at(-2) * PLANE + q
    for peer in (up, down, second_up, second_down):
        pl.semaphore_signal(barrier, inc=1, device_id={"rows": peer}, device_id_type=MESH)

    @pl.loop(1, PLANE)
    def _(p):
        peer = z * PLANE + lax.rem(q + p, PLANE)
        pl.semaphore_signal(barrier, inc=1, device_id={"rows": peer}, device_id_type=MESH)

    pl.semaphore_wait(barrier, PLANE + 3)

    def send(src, dst, ssem, rsem, peer):
        return pltpu.make_async_remote_copy(
            src_ref=src, dst_ref=dst, send_sem=ssem, recv_sem=rsem, device_id={"rows": peer}, device_id_type=MESH
        )

    def z_copies(k, step):
        src_up, dst_up, src_down, dst_down = (
            (own[k], up1[k], own[k], down1[k]),
            (up1[k], up2[k], down1[k], down2[k]),
            (up3s[k], up3[k], down3s[k], down3[k]),
            (up3[k].at[pl.ds(PLANE, 4)], far[k].at[0], down3[k].at[pl.ds(PLANE, 4)], far[k].at[1]),
        )[step]
        i = (k * 4 + step) * 2
        return (
            send(src_up, dst_up, zs.at[i], zr.at[i], up),
            send(src_down, dst_down, zs.at[i + 1], zr.at[i + 1], down),
        )

    def z_start(k, step):
        for copy in z_copies(k, step):
            copy.start()

    def z_wait(k, step):
        for copy in z_copies(k, step):
            copy.wait_recv()

    def block_of(dz_reader, reader, dz_owner):
        return table[at(dz_reader) * PLANE + reader, 0, at(dz_owner) * PLANE + q]

    def plane_rows(dz):
        return pl.ds(at(dz) * PLANE, PLANE)

    def table_copy(i, dz):
        return pltpu.make_async_copy(rows_buf.at[plane_rows(dz)], table.at[plane_rows(dz)], table_sem.at[i])

    hops = ((up, -1), (down, 1), (second_up, -2), (second_down, 2))

    def rows_copy(i):
        src = rows_buf.at[plane_rows(0)]
        return send(src, src, ps.at[1 + i], pr.at[1 + i], hops[i][0])

    def share_plan():
        request, slot, row = plan_rows(me, cols[...], counts[...], own[0].shape[0])
        plan_out[0:1] = slot
        plan_out[1:2] = row
        rows_buf[me] = request

        @pl.loop(1, PLANE)
        def _(p):
            src = rows_buf.at[me]
            send(src, src, ps.at[0], pr.at[0], z * PLANE + lax.rem(q + p, PLANE)).start()

        most = rows_buf.at[pl.ds(0, PLANE - 1)]
        pltpu.make_async_copy(most, most, pr.at[0]).wait()
        for i in range(4):
            rows_copy(i).start()
        table_copy(0, 0).start()
        table_copy(0, 0).wait()

    def take_plan():
        for i, (_, dz) in enumerate(hops):
            src = rows_buf.at[plane_rows(dz)]
            pltpu.make_async_copy(src, src, pr.at[1 + i]).wait()
            table_copy(1 + i, dz).start()
        for i, (_, dz) in enumerate(hops):
            table_copy(1 + i, dz).wait()

    def x_pick(k, first, sources):
        @pl.loop(0, PLANE)
        def _(reader):
            for i, (ref, dz) in enumerate(sources):
                picked[k][reader, first + i] = ref[block_of(0, reader, dz)]

        arrived[k][pl.ds(q * PLANES + first, len(sources))] = picked[k][q, pl.ds(first, len(sources))]

        @pl.loop(1, PLANE)
        def _(p):
            reader = lax.rem(q + p, PLANE)
            send(
                picked[k].at[reader, pl.ds(first, len(sources))],
                arrived[k].at[pl.ds(q * PLANES + first, len(sources))],
                xs.at[k],
                xr.at[k],
                z * PLANE + reader,
            ).start()

    def x_pass(k, first, source):
        arrived[k][q * PLANES + first] = source(q)[...]

        @pl.loop(1, PLANE)
        def _(p):
            reader = lax.rem(q + p, PLANE)
            send(source(reader), arrived[k].at[q * PLANES + first], xs.at[k], xr.at[k], z * PLANE + reader).start()

    def gather_copy(k, i, src, dst, peer):
        j = k * 8 + i
        return send(src, dst, gs.at[j], gr.at[j], peer)

    def mine(k, qq):
        return gathered[k].at[qq]

    def q_of(xx):
        return lax.rem(x + xx + 4, 4) * 2 + c

    def gather_copies(k, i):
        if i == 0:
            src = gathered[k].at[q, 1 - even]
            return gather_copy(k, 0, src, src, partner)
        if i == 1:
            return gather_copy(k, 1, mine(k, q), mine(k, q), right)
        if i == 2:
            return gather_copy(k, 2, mine(k, q), mine(k, q), left)
        if i == 3:
            src = gathered[k].at[q_of(-1), 0]
            return gather_copy(k, 3, src, src, right)
        if i == 4:
            src = gathered[k].at[q_of(1), 1]
            return gather_copy(k, 4, src, src, left)
        src = mine(k, q_of((0, 1, -1)[i - 5])) if i < 8 else None
        return gather_copy(k, i, src, src, other)

    def last_core_copy(k):
        src = mine(k, q_of(2))
        j = PARTS * 8 + k
        return send(src, src, gs.at[j], gr.at[j], other)

    def keep_own(k):
        part = pl.ds(PLANE * PLANES, own[k].shape[0])
        return pltpu.make_async_copy(features.at[:, pl.ds(k * part_rows, part_rows)], arrived[k].at[part], out_sem.at[k])

    def stage(k, s):
        if s == 0:
            load(k).wait()
            z_start(k, 0)
            keep_own(k).start()
            if k == 0:
                share_plan()
            x_pick(k, 0, [(own[k], 0)])
        elif s == 1:
            z_wait(k, 0)
            z_start(k, 1)
            x_pick(k, 1, [(up1[k], -1), (down1[k], 1)])
        elif s == 2:
            z_wait(k, 1)
            if k == 0:
                take_plan()

            @pl.loop(0, PLANE)
            def _(reader):
                up3s[k][reader] = up2[k][block_of(1, reader, -2)]
                down3s[k][reader] = down2[k][block_of(-1, reader, 2)]

            @pl.loop(0, 4)
            def _(half):
                up3s[k][PLANE + half] = up2[k][block_of(2, 2 * half, -2)]
                down3s[k][PLANE + half] = down2[k][block_of(-2, 2 * half + 1, 2)]

            z_start(k, 2)
            x_pick(k, 3, [(up2[k], -2), (down2[k], 2)])
        elif s == 3:
            z_wait(k, 2)
            z_start(k, 3)
            x_pass(k, 5, lambda reader: up3[k].at[reader])
            x_pass(k, 6, lambda reader: down3[k].at[reader])
        elif s == 4:
            z_wait(k, 3)
            x_pass(k, 7, lambda reader: far[k].at[lax.rem(reader, 2), reader // 2])
        elif s == 5:
            everything = arrived[k].at[pl.ds(0, (PLANE - 1) * PLANES)]
            pltpu.make_async_copy(everything, everything, xr.at[k]).wait()
            keep_own(k).wait()
            for i in range(HEAVY):
                gathered[k][q, 1 - even, i] = arrived[k][table[me, 0, PLANES * PLANE + i]]
            gather_copies(k, 0).start()
        elif s == 6:
            gather_copies(k, 0).wait_recv()
            for i in (1, 2, 5):
                gather_copies(k, i).start()
        elif s == 7:
            gather_copies(k, 1).wait_recv()
            gather_copies(k, 2).wait_recv()
            for i in (3, 4, 6, 7):
                gather_copies(k, i).start()
        elif s == 8:
            gather_copies(k, 3).wait_recv()
            gather_copies(k, 4).wait_recv()
            last_core_copy(k).start()
        elif s == 9:
            for i in (5, 6, 7):
                gather_copies(k, i).wait_recv()
            last_core_copy(k).wait_recv()

    for t in range(PARTS + 9):
        for s in range(10):
            if 0 <= t - s < PARTS:
                stage(t - s, s)

    tile_load.wait()
    most = rows_buf.at[pl.ds(0, PLANE - 1)]
    pltpu.make_async_copy(most, most, ps.at[0]).wait()
    for i in range(4):
        rows_copy(i).wait_send()
    for k in range(PARTS):
        for step in range(4):
            for copy in z_copies(k, step):
                copy.wait_send()
        everything = arrived[k].at[pl.ds(0, (PLANE - 1) * PLANES)]
        pltpu.make_async_copy(everything, everything, xs.at[k]).wait()
        for i in range(8):
            gather_copies(k, i).wait_send()
        last_core_copy(k).wait_send()


def exchange(cols, counts, own, tiles):
    blocks, side, feat = own.shape
    rows = side // PARTS
    vmem = pl.BlockSpec(memory_space=pltpu.VMEM)
    anywhere = pl.BlockSpec(memory_space=pl.ANY)
    leads = [(blocks,)] * 5 + [(PLANE + 4,)] * 4 + [(2, 4), (PLANE, 5)]
    bufs = [pltpu.VMEM(lead + (rows, feat), jnp.float32) for lead in leads for _ in range(PARTS)]
    dma = pltpu.SemaphoreType.DMA
    return pl.pallas_call(
        exchange_kernel,
        out_shape=[jax.ShapeDtypeStruct((PLANE * PLANES + blocks, rows, feat), jnp.float32)] * PARTS
        + [jax.ShapeDtypeStruct((PLANE, 2, HEAVY, rows, feat), jnp.float32)] * PARTS
        + [jax.ShapeDtypeStruct((2, cols.shape[1]), jnp.int32), jax.ShapeDtypeStruct(tiles.shape, jnp.float32)],
        in_specs=[vmem, vmem, anywhere, anywhere],
        out_specs=[vmem] * (2 * PARTS + 2),
        scratch_shapes=bufs
        + [
            pltpu.VMEM((PLANE * PLANES, 1, cols.shape[1]), jnp.int32),
            pltpu.SMEM((PLANE * PLANES, 1, cols.shape[1]), jnp.int32),
            dma((PARTS,)),
            dma((PARTS * 8,)),
            dma((PARTS * 8,)),
            dma((PARTS,)),
            dma((PARTS,)),
            dma((PARTS * 9,)),
            dma((PARTS * 9,)),
            dma((PARTS,)),
            dma((5,)),
            dma((5,)),
            dma((5,)),
            dma,
        ],
        compiler_params=pltpu.CompilerParams(collective_id=0, has_side_effects=True, vmem_limit_bytes=25 << 20),
    )(cols, counts, own, tiles)


def per_device(features, norm_gain, row_counts, tile_cols, tile_values):
    node_dev, feat_dev = features.shape
    side = tile_values.shape[1]
    blocks = node_dev // side
    total = tile_values.shape[0]
    own = features.reshape(blocks, side, feat_dev)
    *blocks_got, plan, tiles = exchange(tile_cols.reshape(1, total), row_counts, own, tile_values)
    panel, heavy = blocks_got[:PARTS], [h.reshape((blocks * HEAVY,) + h.shape[-2:]) for h in blocks_got[PARTS:]]
    aggregate = tile_product(plan, tiles, panel, heavy)
    aggregate = aggregate.reshape(node_dev, feat_dev)
    square_sum = lax.psum(jnp.sum(aggregate * aggregate, axis=1), "feat")
    mean_square = square_sum / (feat_dev * lax.axis_size("feat"))
    return aggregate * norm_gain[None, :] * lax.rsqrt(mean_square + 1e-05)[:, None]


def solution(mesh):
    placed = (P("rows", "feat"), P("feat"), P("rows", None), P("rows"), P("rows", None, None))
    return jax.shard_map(
        per_device, mesh=mesh, in_specs=placed, out_specs=P("rows", "feat"), check_vma=False
    )
```

```python
import functools

import jax
import jax.numpy as jnp
from jax import lax
from jax.experimental import pallas as pl
from jax.experimental.pallas import tpu as pltpu
from jax.sharding import PartitionSpec as P

HEAVY = 3
GROUP = 16
TOGETHER = 4


def halves(value):
    high = value.astype(jnp.bfloat16)
    return high, (value - high.astype(jnp.float32)).astype(jnp.bfloat16)


def tile_kernel(plan, tiles, *rest):
    panel, heavy = rest[:PARTS], rest[PARTS : 2 * PARTS]
    out = rest[2 * PARTS]
    total, light = tiles.shape[0], panel[0].shape[0]
    out[...] = jnp.zeros_like(out)

    def product(t):
        slot = plan[0, t]
        is_light, i, j = slot < light, jnp.minimum(slot, light - 1), jnp.maximum(slot - light, 0)
        x = jnp.concatenate([jnp.where(is_light, panel[k][i], heavy[k][j]) for k in range(PARTS)], axis=0)
        x_hi, x_lo = halves(jnp.maximum(x, 0.0))
        a_hi, a_lo = halves(tiles[t])
        return jnp.dot(
            jnp.concatenate([a_hi, a_lo], axis=1),
            jnp.concatenate([x_hi, x_hi], axis=0),
            preferred_element_type=jnp.float32,
        ) + jnp.dot(a_hi, x_lo, preferred_element_type=jnp.float32)

    @pl.loop(0, total // TOGETHER)
    def _(step):
        ts = [step * TOGETHER + u for u in range(TOGETHER)]
        products = [product(t) for t in ts]
        for t, prod in zip(ts, products):
            out[plan[1, t]] += prod


def tile_product(plan, tiles, panel, heavy):
    side = tiles.shape[1]
    blocks, feat = panel[0].shape[0] - PLANE * PLANES, panel[0].shape[-1]
    vmem = pl.BlockSpec(memory_space=pltpu.VMEM)
    return pl.pallas_call(
        tile_kernel,
        out_shape=jax.ShapeDtypeStruct((blocks, side, feat), jnp.float32),
        in_specs=[pl.BlockSpec(memory_space=pltpu.SMEM)] + [vmem] * (2 * PARTS + 1),
        out_specs=vmem,
        compiler_params=pltpu.CompilerParams(vmem_limit_bytes=8 << 20),
    )(plan, tiles, *panel, *heavy)


PARTS = 8
PLANE = 8
PLANES = 8
ORDER = ((0, 0), (1, 1), (2, 2), (3, 3), (4, 4), (5, 5), (6, 6), (7, 7), (8, 8), (9, 9))
MESH = pl.DeviceIdType.MESH


def total_of(mask, values, axis):
    return jnp.sum(jnp.where(mask, values, 0), axis=axis, keepdims=True)


def plan_rows(me, cols, counts, blocks):
    lanes = cols.shape[1]
    devices, shift = PLANE * PLANES, blocks.bit_length() - 1
    i = lax.broadcasted_iota(jnp.int32, (lanes, lanes), 0)
    j = lax.broadcasted_iota(jnp.int32, (lanes, lanes), 1)
    lane, down = j[:1], i[:, :1]

    def panel_slot(stripe):
        ahead = ((stripe >> 3) - me // PLANE + PLANES) & (PLANES - 1)
        return (stripe & (PLANE - 1)) * PLANES + jnp.where(ahead < 4, 2 * ahead, 2 * (PLANES - ahead) - 1)

    spread = jnp.broadcast_to(cols, (lanes, lanes))
    turned = spread.T
    hit = (turned >> shift) == j
    wanted = jnp.max(jnp.where(hit, turned & (blocks - 1), 0), axis=0, keepdims=True)
    marked = (total_of(hit, 1, 0) >= 2) & (lane != me)
    i_am_heavy = total_of(marked, 1, 1) < HEAVY
    marked = marked | ((lane == me) & i_am_heavy)
    hit_down = (spread >> shift) == i
    marked_down = (total_of(hit_down, 1, 1) >= 2) & (down != me)
    marked_down = marked_down | ((down == me) & i_am_heavy)
    rank = total_of(jnp.broadcast_to(marked_down, i.shape) & (i < j), 1, 0)
    rank_down = total_of(jnp.broadcast_to(marked, i.shape) & (j < i), 1, 1)
    request = jnp.where(marked | (lane == me), me & (GROUP - 1), wanted)
    for s in range(HEAVY):
        request = jnp.where(lane == devices + s, total_of(marked & (rank == s), panel_slot(lane), 1), request)
    heavy_hit = hit_down & marked_down
    local = cols & (blocks - 1)
    slot = jnp.where(
        total_of(heavy_hit, 1, 0) > 0,
        devices + blocks + ((local & (PLANE - 1)) * 2 + (local >> 3)) * HEAVY + total_of(heavy_hit, jnp.broadcast_to(rank_down, i.shape), 0),
        panel_slot(cols >> shift),
    )
    slot = jnp.where((cols >> shift) == me, devices + local, slot)
    side = counts.shape[1]
    ends = total_of(j[:side, :side] <= i[:side, :side], jnp.broadcast_to(counts, (side, side)), 1)
    row = total_of(ends <= j[:side], 1, 0)
    return request, slot, row


def exchange_kernel(cols, counts, features, tiles, *rest):
    arrived, gathered = rest[:PARTS], rest[PARTS : 2 * PARTS]
    plan_out, tiles_out, scratch = rest[2 * PARTS], rest[2 * PARTS + 1], rest[2 * PARTS + 2 :]
    names = ("own", "up1", "down1", "up2", "down2", "up3s", "down3s", "up3", "down3", "far", "picked")
    bufs = {n: scratch[i * PARTS : (i + 1) * PARTS] for i, n in enumerate(names)}
    own, up1, down1, up2, down2, up3s, down3s, up3, down3, far, picked = (bufs[n] for n in names)
    (rows_buf, table, load_sem, zs, zr, xs, xr, gs, gr, out_sem, ps, pr, table_sem, tile_sem, cols_buf, counts_buf, small_sem) = scratch[len(names) * PARTS :]
    me = lax.axis_index("rows")
    z, q = me // PLANE, lax.rem(me, PLANE)
    x, c = q // 2, lax.rem(q, 2)
    part_rows = own[0].shape[1]

    def at(dz):
        return lax.rem(z + dz + PLANES, PLANES)

    up, down = at(1) * PLANE + q, at(-1) * PLANE + q
    even = 1 - lax.rem(z, 2)
    partner = (z + 2 * even - 1) * PLANE + q
    right = z * PLANE + lax.rem(x + 1, 4) * 2 + c
    left = z * PLANE + lax.rem(x + 3, 4) * 2 + c
    other = z * PLANE + x * 2 + 1 - c

    def load(k):
        return pltpu.make_async_copy(features.at[:, pl.ds(k * part_rows, part_rows)], own[k], load_sem.at[k])

    for k in range(PARTS):
        load(k).start()
    small_loads = (
        pltpu.make_async_copy(cols, cols_buf, small_sem.at[0]),
        pltpu.make_async_copy(counts, counts_buf, small_sem.at[1]),
    )
    for copy in small_loads:
        copy.start()
    tile_load = pltpu.make_async_copy(tiles, tiles_out, tile_sem)
    tile_load.start()
    barrier = pltpu.get_barrier_semaphore()
    second_up, second_down = at(2) * PLANE + q, at(-2) * PLANE + q
    for peer in (up, down, second_up, second_down):
        pl.semaphore_signal(barrier, inc=1, device_id={"rows": peer}, device_id_type=MESH)

    @pl.loop(1, PLANE)
    def _(p):
        peer = z * PLANE + lax.rem(q + p, PLANE)
        pl.semaphore_signal(barrier, inc=1, device_id={"rows": peer}, device_id_type=MESH)

    pl.semaphore_wait(barrier, PLANE + 3)

    def send(src, dst, ssem, rsem, peer):
        return pltpu.make_async_remote_copy(
            src_ref=src, dst_ref=dst, send_sem=ssem, recv_sem=rsem, device_id={"rows": peer}, device_id_type=MESH
        )

    def z_copies(k, step):
        src_up, dst_up, src_down, dst_down = (
            (own[k], up1[k], own[k], down1[k]),
            (up1[k], up2[k], down1[k], down2[k]),
            (up3s[k], up3[k], down3s[k], down3[k]),
            (up3[k].at[pl.ds(PLANE, 4)], far[k].at[0], down3[k].at[pl.ds(PLANE, 4)], far[k].at[1]),
        )[step]
        i = (k * 4 + step) * 2
        return (
            send(src_up, dst_up, zs.at[i], zr.at[i], up),
            send(src_down, dst_down, zs.at[i + 1], zr.at[i + 1], down),
        )

    def z_start(k, step):
        for copy in z_copies(k, step):
            copy.start()

    def z_wait(k, step):
        for copy in z_copies(k, step):
            copy.wait_recv()

    def block_of(dz_reader, reader, dz_owner):
        return table[at(dz_reader) * PLANE + reader, 0, at(dz_owner) * PLANE + q]

    def plane_rows(dz):
        return pl.ds(at(dz) * PLANE, PLANE)

    def table_copy(i, dz):
        return pltpu.make_async_copy(rows_buf.at[plane_rows(dz)], table.at[plane_rows(dz)], table_sem.at[i])

    hops = ((up, -1), (down, 1), (second_up, -2), (second_down, 2))

    def rows_copy(i):
        src = rows_buf.at[plane_rows(0)]
        return send(src, src, ps.at[1 + i], pr.at[1 + i], hops[i][0])

    def share_plan():
        for copy in small_loads:
            copy.wait()
        request, slot, row = plan_rows(me, cols_buf[...], counts_buf[...], own[0].shape[0])
        plan_out[0:1] = slot
        plan_out[1:2] = row
        rows_buf[me] = request

        @pl.loop(1, PLANE)
        def _(p):
            src = rows_buf.at[me]
            send(src, src, ps.at[0], pr.at[0], z * PLANE + lax.rem(q + p, PLANE)).start()

        most = rows_buf.at[pl.ds(0, PLANE - 1)]
        pltpu.make_async_copy(most, most, pr.at[0]).wait()
        for i in range(4):
            rows_copy(i).start()
        table_copy(0, 0).start()
        table_copy(0, 0).wait()

    def take_plan():
        for i, (_, dz) in enumerate(hops):
            src = rows_buf.at[plane_rows(dz)]
            pltpu.make_async_copy(src, src, pr.at[1 + i]).wait()
            table_copy(1 + i, dz).start()
        for i, (_, dz) in enumerate(hops):
            table_copy(1 + i, dz).wait()

    def x_pick(k, first, sources):
        @pl.loop(0, PLANE)
        def _(reader):
            for i, (ref, dz) in enumerate(sources):
                picked[k][reader, first + i] = ref[block_of(0, reader, dz)]

        arrived[k][pl.ds(q * PLANES + first, len(sources))] = picked[k][q, pl.ds(first, len(sources))]

        @pl.loop(1, PLANE)
        def _(p):
            reader = lax.rem(q + p, PLANE)
            send(
                picked[k].at[reader, pl.ds(first, len(sources))],
                arrived[k].at[pl.ds(q * PLANES + first, len(sources))],
                xs.at[k],
                xr.at[k],
                z * PLANE + reader,
            ).start()

    def x_pass(k, first, source):
        arrived[k][q * PLANES + first] = source(q)[...]

        @pl.loop(1, PLANE)
        def _(p):
            reader = lax.rem(q + p, PLANE)
            send(source(reader), arrived[k].at[q * PLANES + first], xs.at[k], xr.at[k], z * PLANE + reader).start()

    def gather_copy(k, i, src, dst, peer):
        j = k * 8 + i
        return send(src, dst, gs.at[j], gr.at[j], peer)

    def mine(k, qq):
        return gathered[k].at[qq]

    def q_of(xx):
        return lax.rem(x + xx + 4, 4) * 2 + c

    def gather_copies(k, i):
        if i == 0:
            src = gathered[k].at[q, 1 - even]
            return gather_copy(k, 0, src, src, partner)
        if i == 1:
            return gather_copy(k, 1, mine(k, q), mine(k, q), right)
        if i == 2:
            return gather_copy(k, 2, mine(k, q), mine(k, q), left)
        if i == 3:
            src = gathered[k].at[q_of(-1), 0]
            return gather_copy(k, 3, src, src, right)
        if i == 4:
            src = gathered[k].at[q_of(1), 1]
            return gather_copy(k, 4, src, src, left)
        src = mine(k, q_of((0, 1, -1)[i - 5])) if i < 8 else None
        return gather_copy(k, i, src, src, other)

    def last_core_copy(k):
        src = mine(k, q_of(2))
        j = PARTS * 8 + k
        return send(src, src, gs.at[j], gr.at[j], other)

    def keep_own(k):
        part = pl.ds(PLANE * PLANES, own[k].shape[0])
        return pltpu.make_async_copy(features.at[:, pl.ds(k * part_rows, part_rows)], arrived[k].at[part], out_sem.at[k])

    def stage(k, s):
        if s == 0:
            load(k).wait()
            z_start(k, 0)
            keep_own(k).start()
            if k == 0:
                share_plan()
            x_pick(k, 0, [(own[k], 0)])
        elif s == 1:
            z_wait(k, 0)
            z_start(k, 1)
            x_pick(k, 1, [(up1[k], -1), (down1[k], 1)])
        elif s == 2:
            z_wait(k, 1)
            if k == 0:
                take_plan()

            @pl.loop(0, PLANE)
            def _(reader):
                up3s[k][reader] = up2[k][block_of(1, reader, -2)]
                down3s[k][reader] = down2[k][block_of(-1, reader, 2)]

            @pl.loop(0, 4)
            def _(half):
                up3s[k][PLANE + half] = up2[k][block_of(2, 2 * half, -2)]
                down3s[k][PLANE + half] = down2[k][block_of(-2, 2 * half + 1, 2)]

            z_start(k, 2)
            x_pick(k, 3, [(up2[k], -2), (down2[k], 2)])
        elif s == 3:
            z_wait(k, 2)
            z_start(k, 3)
            x_pass(k, 5, lambda reader: up3[k].at[reader])
            x_pass(k, 6, lambda reader: down3[k].at[reader])
        elif s == 4:
            z_wait(k, 3)
            x_pass(k, 7, lambda reader: far[k].at[lax.rem(reader, 2), reader // 2])
        elif s == 5:
            everything = arrived[k].at[pl.ds(0, (PLANE - 1) * PLANES)]
            pltpu.make_async_copy(everything, everything, xr.at[k]).wait()
            keep_own(k).wait()
            for i in range(HEAVY):
                gathered[k][q, 1 - even, i] = arrived[k][table[me, 0, PLANES * PLANE + i]]
            gather_copies(k, 0).start()
        elif s == 6:
            gather_copies(k, 0).wait_recv()
            for i in (1, 2, 5):
                gather_copies(k, i).start()
        elif s == 7:
            gather_copies(k, 1).wait_recv()
            gather_copies(k, 2).wait_recv()
            for i in (3, 4, 6, 7):
                gather_copies(k, i).start()
        elif s == 8:
            gather_copies(k, 3).wait_recv()
            gather_copies(k, 4).wait_recv()
            last_core_copy(k).start()
        elif s == 9:
            for i in (5, 6, 7):
                gather_copies(k, i).wait_recv()
            last_core_copy(k).wait_recv()

    for t in range(PARTS + 9):
        for s, lag in ORDER:
            if 0 <= t - lag < PARTS:
                stage(t - lag, s)

    tile_load.wait()
    most = rows_buf.at[pl.ds(0, PLANE - 1)]
    pltpu.make_async_copy(most, most, ps.at[0]).wait()
    for i in range(4):
        rows_copy(i).wait_send()
    for k in range(PARTS):
        for step in range(4):
            for copy in z_copies(k, step):
                copy.wait_send()
        everything = arrived[k].at[pl.ds(0, (PLANE - 1) * PLANES)]
        pltpu.make_async_copy(everything, everything, xs.at[k]).wait()
        for i in range(8):
            gather_copies(k, i).wait_send()
        last_core_copy(k).wait_send()


def exchange(cols, counts, own, tiles):
    blocks, side, feat = own.shape
    rows = side // PARTS
    vmem = pl.BlockSpec(memory_space=pltpu.VMEM)
    hbm = pl.BlockSpec(memory_space=pltpu.HBM)
    leads = [(blocks,)] * 5 + [(PLANE + 4,)] * 4 + [(2, 4), (PLANE, 5)]
    bufs = [pltpu.VMEM(lead + (rows, feat), jnp.float32) for lead in leads for _ in range(PARTS)]
    dma = pltpu.SemaphoreType.DMA
    return pl.pallas_call(
        exchange_kernel,
        out_shape=[jax.ShapeDtypeStruct((PLANE * PLANES + blocks, rows, feat), jnp.float32)] * PARTS
        + [jax.ShapeDtypeStruct((PLANE, 2, HEAVY, rows, feat), jnp.float32)] * PARTS
        + [jax.ShapeDtypeStruct((2, cols.shape[1]), jnp.int32), jax.ShapeDtypeStruct(tiles.shape, jnp.float32)],
        in_specs=[hbm] * 4,
        out_specs=[vmem] * (2 * PARTS + 2),
        scratch_shapes=bufs
        + [
            pltpu.VMEM((PLANE * PLANES, 1, cols.shape[1]), jnp.int32),
            pltpu.SMEM((PLANE * PLANES, 1, cols.shape[1]), jnp.int32),
            dma((PARTS,)),
            dma((PARTS * 8,)),
            dma((PARTS * 8,)),
            dma((PARTS,)),
            dma((PARTS,)),
            dma((PARTS * 9,)),
            dma((PARTS * 9,)),
            dma((PARTS,)),
            dma((5,)),
            dma((5,)),
            dma((5,)),
            dma,
            pltpu.VMEM(cols.shape, jnp.int32),
            pltpu.VMEM(counts.shape, jnp.int32),
            dma((2,)),
        ],
        compiler_params=pltpu.CompilerParams(collective_id=0, has_side_effects=True, vmem_limit_bytes=25 << 20),
    )(cols, counts, own, tiles)


def feat_sum_kernel(share, out, held, ss, rs):
    me, size = lax.axis_index("feat"), held.shape[0]
    peers = [lax.rem(me + p, size) for p in range(1, size)]
    barrier = pltpu.get_barrier_semaphore()
    for peer in peers:
        pl.semaphore_signal(barrier, inc=1, device_id={"feat": peer}, device_id_type=MESH)
    held[me] = share[...]
    pl.semaphore_wait(barrier, size - 1)
    copies = [
        pltpu.make_async_remote_copy(
            src_ref=held.at[me],
            dst_ref=held.at[me],
            send_sem=ss.at[i],
            recv_sem=rs.at[i],
            device_id={"feat": peer},
            device_id_type=MESH,
        )
        for i, peer in enumerate(peers)
    ]
    for copy in copies:
        copy.start()
    for copy in copies:
        copy.wait()
    out[...] = sum(held[i] for i in range(size))


def feat_sum(share):
    size = lax.axis_size("feat")
    vmem = pl.BlockSpec(memory_space=pltpu.VMEM)
    return pl.pallas_call(
        feat_sum_kernel,
        out_shape=jax.ShapeDtypeStruct(share.shape, jnp.float32),
        in_specs=[vmem],
        out_specs=vmem,
        scratch_shapes=[
            pltpu.VMEM((size,) + share.shape, jnp.float32),
            pltpu.SemaphoreType.DMA((size - 1,)),
            pltpu.SemaphoreType.DMA((size - 1,)),
        ],
        compiler_params=pltpu.CompilerParams(collective_id=1, has_side_effects=True, vmem_limit_bytes=2 << 20),
    )(share)


def per_device(features, norm_gain, row_counts, tile_cols, tile_values):
    node_dev, feat_dev = features.shape
    side = tile_values.shape[1]
    blocks = node_dev // side
    total = tile_values.shape[0]
    own = features.reshape(blocks, side, feat_dev)
    *blocks_got, plan, tiles = exchange(tile_cols.reshape(1, total), row_counts, own, tile_values)
    panel, heavy = blocks_got[:PARTS], [h.reshape((blocks * HEAVY,) + h.shape[-2:]) for h in blocks_got[PARTS:]]
    aggregate = tile_product(plan, tiles, panel, heavy)
    square_sum = feat_sum(jnp.sum(aggregate * aggregate, axis=2))
    mean_square = square_sum / (feat_dev * lax.axis_size("feat"))
    normed = aggregate * norm_gain[None, None, :] * lax.rsqrt(mean_square + 1e-05)[:, :, None]
    return normed.reshape(node_dev, feat_dev)


def solution(mesh):
    placed = (P("rows", "feat"), P("feat"), P("rows", None), P("rows"), P("rows", None, None))
    return jax.shard_map(
        per_device, mesh=mesh, in_specs=placed, out_specs=P("rows", "feat"), check_vma=False
    )
```

```python
import functools

import jax
import jax.numpy as jnp
from jax import lax
from jax.experimental import pallas as pl
from jax.experimental.pallas import tpu as pltpu
from jax.sharding import PartitionSpec as P

HEAVY = 3
GROUP = 16
TOGETHER = 4


def halves(value):
    high = value.astype(jnp.bfloat16)
    return high, (value - high.astype(jnp.float32)).astype(jnp.bfloat16)


def tile_kernel(plan, tiles, *rest):
    panel, heavy = rest[:PARTS], rest[PARTS : 2 * PARTS]
    out = rest[2 * PARTS]
    total, light = tiles.shape[0], panel[0].shape[0]
    out[...] = jnp.zeros_like(out)

    def product(t):
        slot = plan[0, t]
        is_light, i, j = slot < light, jnp.minimum(slot, light - 1), jnp.maximum(slot - light, 0)
        x = jnp.concatenate([jnp.where(is_light, panel[k][i], heavy[k][j]) for k in range(PARTS)], axis=0)
        x_hi, x_lo = halves(jnp.maximum(x, 0.0))
        a_hi, a_lo = halves(tiles[t])
        return jnp.dot(
            jnp.concatenate([a_hi, a_lo], axis=1),
            jnp.concatenate([x_hi, x_hi], axis=0),
            preferred_element_type=jnp.float32,
        ) + jnp.dot(a_hi, x_lo, preferred_element_type=jnp.float32)

    @pl.loop(0, total // TOGETHER)
    def _(step):
        ts = [step * TOGETHER + u for u in range(TOGETHER)]
        products = [product(t) for t in ts]
        for t, prod in zip(ts, products):
            out[plan[1, t]] += prod


def tile_product(plan, tiles, panel, heavy):
    side = tiles.shape[1]
    blocks, feat = panel[0].shape[0] - PLANE * PLANES, panel[0].shape[-1]
    vmem = pl.BlockSpec(memory_space=pltpu.VMEM)
    return pl.pallas_call(
        tile_kernel,
        out_shape=jax.ShapeDtypeStruct((blocks, side, feat), jnp.float32),
        in_specs=[pl.BlockSpec(memory_space=pltpu.SMEM)] + [vmem] * (2 * PARTS + 1),
        out_specs=vmem,
        compiler_params=pltpu.CompilerParams(vmem_limit_bytes=8 << 20),
    )(plan, tiles, *panel, *heavy)


PARTS = 8
PLANE = 8
PLANES = 8
ORDER = tuple((stage, stage) for stage in range(10))
MESH = pl.DeviceIdType.MESH


def total_of(mask, values, axis):
    return jnp.sum(jnp.where(mask, values, 0), axis=axis, keepdims=True)


def plan_rows(me, cols, counts, blocks):
    lanes = cols.shape[1]
    devices, shift = PLANE * PLANES, blocks.bit_length() - 1
    i = lax.broadcasted_iota(jnp.int32, (lanes, lanes), 0)
    j = lax.broadcasted_iota(jnp.int32, (lanes, lanes), 1)
    lane, down = j[:1], i[:, :1]

    def panel_slot(stripe):
        ahead = ((stripe >> 3) - me // PLANE + PLANES) & (PLANES - 1)
        return (stripe & (PLANE - 1)) * PLANES + jnp.where(ahead < 4, 2 * ahead, 2 * (PLANES - ahead) - 1)

    spread = jnp.broadcast_to(cols, (lanes, lanes))
    turned = spread.T
    hit = (turned >> shift) == j
    wanted = jnp.max(jnp.where(hit, turned & (blocks - 1), 0), axis=0, keepdims=True)
    marked = (total_of(hit, 1, 0) >= 2) & (lane != me)
    i_am_heavy = total_of(marked, 1, 1) < HEAVY
    marked = marked | ((lane == me) & i_am_heavy)
    hit_down = (spread >> shift) == i
    marked_down = (total_of(hit_down, 1, 1) >= 2) & (down != me)
    marked_down = marked_down | ((down == me) & i_am_heavy)
    rank = total_of(jnp.broadcast_to(marked_down, i.shape) & (i < j), 1, 0)
    rank_down = total_of(jnp.broadcast_to(marked, i.shape) & (j < i), 1, 1)
    request = jnp.where(marked | (lane == me), me & (GROUP - 1), wanted)
    for s in range(HEAVY):
        request = jnp.where(lane == devices + s, total_of(marked & (rank == s), panel_slot(lane), 1), request)
    heavy_hit = hit_down & marked_down
    local = cols & (blocks - 1)
    slot = jnp.where(
        total_of(heavy_hit, 1, 0) > 0,
        devices + blocks + ((local & (PLANE - 1)) * 2 + (local >> 3)) * HEAVY + total_of(heavy_hit, jnp.broadcast_to(rank_down, i.shape), 0),
        panel_slot(cols >> shift),
    )
    slot = jnp.where((cols >> shift) == me, devices + local, slot)
    side = counts.shape[1]
    ends = total_of(j[:side, :side] <= i[:side, :side], jnp.broadcast_to(counts, (side, side)), 1)
    row = total_of(ends <= j[:side], 1, 0)
    return request, slot, row


def exchange_kernel(cols, counts, features, tiles, *rest):
    arrived, gathered = rest[:PARTS], rest[PARTS : 2 * PARTS]
    plan_out, tiles_out, scratch = rest[2 * PARTS], rest[2 * PARTS + 1], rest[2 * PARTS + 2 :]
    names = ("own", "up1", "down1", "up2", "down2", "up3s", "down3s", "up3", "down3", "far", "picked")
    bufs = {n: scratch[i * PARTS : (i + 1) * PARTS] for i, n in enumerate(names)}
    own, up1, down1, up2, down2, up3s, down3s, up3, down3, far, picked = (bufs[n] for n in names)
    (rows_buf, table, load_sem, zs, zr, xs, xr, gs, gr, out_sem, ps, pr, table_sem, tile_sem, cols_buf, counts_buf, small_sem) = scratch[len(names) * PARTS :]
    me = lax.axis_index("rows")
    z, q = me // PLANE, lax.rem(me, PLANE)
    x, c = q // 2, lax.rem(q, 2)
    part_rows = own[0].shape[1]

    def at(dz):
        return lax.rem(z + dz + PLANES, PLANES)

    up, down = at(1) * PLANE + q, at(-1) * PLANE + q
    even = 1 - lax.rem(z, 2)
    partner = (z + 2 * even - 1) * PLANE + q
    right = z * PLANE + lax.rem(x + 1, 4) * 2 + c
    left = z * PLANE + lax.rem(x + 3, 4) * 2 + c
    other = z * PLANE + x * 2 + 1 - c

    def load(k):
        return pltpu.make_async_copy(features.at[:, pl.ds(k * part_rows, part_rows)], own[k], load_sem.at[k])

    for k in range(PARTS):
        load(k).start()
    small_loads = (
        pltpu.make_async_copy(cols, cols_buf, small_sem.at[0]),
        pltpu.make_async_copy(counts, counts_buf, small_sem.at[1]),
    )
    for copy in small_loads:
        copy.start()
    tile_load = pltpu.make_async_copy(tiles, tiles_out, tile_sem)
    tile_load.start()
    barrier = pltpu.get_barrier_semaphore()
    second_up, second_down = at(2) * PLANE + q, at(-2) * PLANE + q
    for peer in (up, down, second_up, second_down):
        pl.semaphore_signal(barrier, inc=1, device_id={"rows": peer}, device_id_type=MESH)

    @pl.loop(1, PLANE)
    def _(p):
        peer = z * PLANE + lax.rem(q + p, PLANE)
        pl.semaphore_signal(barrier, inc=1, device_id={"rows": peer}, device_id_type=MESH)

    pl.semaphore_wait(barrier, PLANE + 3)

    def send(src, dst, ssem, rsem, peer):
        return pltpu.make_async_remote_copy(
            src_ref=src, dst_ref=dst, send_sem=ssem, recv_sem=rsem, device_id={"rows": peer}, device_id_type=MESH
        )

    def z_copies(k, step):
        src_up, dst_up, src_down, dst_down = (
            (own[k], up1[k], own[k], down1[k]),
            (up1[k], up2[k], down1[k], down2[k]),
            (up3s[k], up3[k], down3s[k], down3[k]),
            (up3[k].at[pl.ds(PLANE, 4)], far[k].at[0], down3[k].at[pl.ds(PLANE, 4)], far[k].at[1]),
        )[step]
        i = (k * 4 + step) * 2
        return (
            send(src_up, dst_up, zs.at[i], zr.at[i], up),
            send(src_down, dst_down, zs.at[i + 1], zr.at[i + 1], down),
        )

    def z_start(k, step):
        for copy in z_copies(k, step):
            copy.start()

    def z_wait(k, step):
        for copy in z_copies(k, step):
            copy.wait_recv()

    def block_of(dz_reader, reader, dz_owner):
        return table[at(dz_reader) * PLANE + reader, 0, at(dz_owner) * PLANE + q]

    def plane_rows(dz):
        return pl.ds(at(dz) * PLANE, PLANE)

    def table_copy(i, dz):
        return pltpu.make_async_copy(rows_buf.at[plane_rows(dz)], table.at[plane_rows(dz)], table_sem.at[i])

    hops = ((up, -1), (down, 1), (second_up, -2), (second_down, 2))

    def rows_copy(i):
        src = rows_buf.at[plane_rows(0)]
        return send(src, src, ps.at[1 + i], pr.at[1 + i], hops[i][0])

    def share_plan():
        for copy in small_loads:
            copy.wait()
        request, slot, row = plan_rows(me, cols_buf[...], counts_buf[...], own[0].shape[0])
        plan_out[0:1] = slot
        plan_out[1:2] = row
        rows_buf[me] = request

        @pl.loop(1, PLANE)
        def _(p):
            src = rows_buf.at[me]
            send(src, src, ps.at[0], pr.at[0], z * PLANE + lax.rem(q + p, PLANE)).start()

        most = rows_buf.at[pl.ds(0, PLANE - 1)]
        pltpu.make_async_copy(most, most, pr.at[0]).wait()
        for i in range(4):
            rows_copy(i).start()
        table_copy(0, 0).start()
        table_copy(0, 0).wait()

    def take_plan():
        for i, (_, dz) in enumerate(hops):
            src = rows_buf.at[plane_rows(dz)]
            pltpu.make_async_copy(src, src, pr.at[1 + i]).wait()
            table_copy(1 + i, dz).start()
        for i, (_, dz) in enumerate(hops):
            table_copy(1 + i, dz).wait()

    def x_pick(k, first, sources):
        @pl.loop(0, PLANE)
        def _(reader):
            for i, (ref, dz) in enumerate(sources):
                picked[k][reader, first + i] = ref[block_of(0, reader, dz)]

        arrived[k][pl.ds(q * PLANES + first, len(sources))] = picked[k][q, pl.ds(first, len(sources))]

        @pl.loop(1, PLANE)
        def _(p):
            reader = lax.rem(q + p, PLANE)
            send(
                picked[k].at[reader, pl.ds(first, len(sources))],
                arrived[k].at[pl.ds(q * PLANES + first, len(sources))],
                xs.at[k],
                xr.at[k],
                z * PLANE + reader,
            ).start()

    def x_pass(k, first, source):
        arrived[k][q * PLANES + first] = source(q)[...]

        @pl.loop(1, PLANE)
        def _(p):
            reader = lax.rem(q + p, PLANE)
            send(source(reader), arrived[k].at[q * PLANES + first], xs.at[k], xr.at[k], z * PLANE + reader).start()

    def q_of(xx):
        return lax.rem(x + xx + 4, 4) * 2 + c

    def pieces_copy(k, i, qq, part, peer):
        piece = gathered[k].at[qq, part]
        return send(piece, piece, gs.at[k * 15 + i], gr.at[k * 15 + i], peer)

    def to_partner(k):
        return pieces_copy(k, 14, q, 1 - even, partner)

    def over_x(k, p):
        part = even if p else 1 - even
        return [pieces_copy(k, p * 7 + i, q, part, peer) for i, peer in enumerate((right, left))]

    def across(k, p):
        return pieces_copy(k, p * 7 + 2, q_of(1 if p else -1), even if p else 1 - even, left if p else right)

    def to_core(k, p):
        part = even if p else 1 - even
        return [pieces_copy(k, p * 7 + 3 + i, q_of(xx), part, other) for i, xx in enumerate((0, -1, 1, 2))]

    def keep_own(k):
        part = pl.ds(PLANE * PLANES, own[k].shape[0])
        return pltpu.make_async_copy(features.at[:, pl.ds(k * part_rows, part_rows)], arrived[k].at[part], out_sem.at[k])

    def z_first(k):
        load(k).wait()
        z_start(k, 0)

    def stage(k, s):
        if s == 0:
            if k == 0:
                z_first(0)
                share_plan()
                for part in range(PARTS):
                    if part == 1:
                        z_first(1)
                    elif part:
                        load(part).wait()
                    keep_own(part).start()
                    x_pick(part, 0, [(own[part], 0)])
            elif k > 1:
                z_start(k, 0)
        elif s == 1:
            z_wait(k, 0)
            z_start(k, 1)
            x_pick(k, 1, [(up1[k], -1), (down1[k], 1)])
        elif s == 2:
            z_wait(k, 1)
            if k == 0:
                take_plan()

            @pl.loop(0, PLANE)
            def _(reader):
                up3s[k][reader] = up2[k][block_of(1, reader, -2)]
                down3s[k][reader] = down2[k][block_of(-1, reader, 2)]

            @pl.loop(0, 4)
            def _(half):
                up3s[k][PLANE + half] = up2[k][block_of(2, 2 * half, -2)]
                down3s[k][PLANE + half] = down2[k][block_of(-2, 2 * half + 1, 2)]

            z_start(k, 2)
            x_pick(k, 3, [(up2[k], -2), (down2[k], 2)])
        elif s == 3:
            z_wait(k, 2)
            z_start(k, 3)
            x_pass(k, 5, lambda reader: up3[k].at[reader])
            x_pass(k, 6, lambda reader: down3[k].at[reader])
        elif s == 4:
            z_wait(k, 3)
            x_pass(k, 7, lambda reader: far[k].at[lax.rem(reader, 2), reader // 2])
        elif s == 5:
            everything = arrived[k].at[pl.ds(0, (PLANE - 1) * PLANES)]
            pltpu.make_async_copy(everything, everything, xr.at[k]).wait()
            keep_own(k).wait()
            for i in range(HEAVY):
                gathered[k][q, 1 - even, i] = arrived[k][table[me, 0, PLANES * PLANE + i]]
            for copy in [to_partner(k)] + over_x(k, 0) + to_core(k, 0)[:1]:
                copy.start()
        elif s == 6:
            to_partner(k).wait_recv()
            for copy in over_x(k, 1) + to_core(k, 1)[:1]:
                copy.start()
            for came in over_x(k, 0):
                came.wait_recv()
            for copy in [across(k, 0)] + to_core(k, 0)[1:3]:
                copy.start()
        elif s == 7:
            for came in over_x(k, 1):
                came.wait_recv()
            for copy in [across(k, 1)] + to_core(k, 1)[1:3]:
                copy.start()
            across(k, 0).wait_recv()
            to_core(k, 0)[3].start()
        elif s == 8:
            across(k, 1).wait_recv()
            to_core(k, 1)[3].start()
        elif s == 9:
            for copy in to_core(k, 0) + to_core(k, 1):
                copy.wait_recv()

    for t in range(PARTS + 9):
        for s, lag in ORDER:
            if 0 <= t - lag < PARTS:
                stage(t - lag, s)

    tile_load.wait()
    most = rows_buf.at[pl.ds(0, PLANE - 1)]
    pltpu.make_async_copy(most, most, ps.at[0]).wait()
    for i in range(4):
        rows_copy(i).wait_send()
    for k in range(PARTS):
        for step in range(4):
            for copy in z_copies(k, step):
                copy.wait_send()
        everything = arrived[k].at[pl.ds(0, (PLANE - 1) * PLANES)]
        pltpu.make_async_copy(everything, everything, xs.at[k]).wait()
        for copy in [to_partner(k)] + over_x(k, 0) + over_x(k, 1) + [across(k, 0), across(k, 1)] + to_core(k, 0) + to_core(k, 1):
            copy.wait_send()


def exchange(cols, counts, own, tiles):
    blocks, side, feat = own.shape
    rows = side // PARTS
    vmem = pl.BlockSpec(memory_space=pltpu.VMEM)
    hbm = pl.BlockSpec(memory_space=pltpu.HBM)
    leads = [(blocks,)] * 5 + [(PLANE + 4,)] * 4 + [(2, 4), (PLANE, 5)]
    bufs = [pltpu.VMEM(lead + (rows, feat), jnp.float32) for lead in leads for _ in range(PARTS)]
    dma = pltpu.SemaphoreType.DMA
    return pl.pallas_call(
        exchange_kernel,
        out_shape=[jax.ShapeDtypeStruct((PLANE * PLANES + blocks, rows, feat), jnp.float32)] * PARTS
        + [jax.ShapeDtypeStruct((PLANE, 2, HEAVY, rows, feat), jnp.float32)] * PARTS
        + [jax.ShapeDtypeStruct((2, cols.shape[1]), jnp.int32), jax.ShapeDtypeStruct(tiles.shape, jnp.float32)],
        in_specs=[hbm] * 4,
        out_specs=[vmem] * (2 * PARTS + 2),
        scratch_shapes=bufs
        + [
            pltpu.VMEM((PLANE * PLANES, 1, cols.shape[1]), jnp.int32),
            pltpu.SMEM((PLANE * PLANES, 1, cols.shape[1]), jnp.int32),
            dma((PARTS,)),
            dma((PARTS * 8,)),
            dma((PARTS * 8,)),
            dma((PARTS,)),
            dma((PARTS,)),
            dma((PARTS * 15,)),
            dma((PARTS * 15,)),
            dma((PARTS,)),
            dma((5,)),
            dma((5,)),
            dma((5,)),
            dma,
            pltpu.VMEM(cols.shape, jnp.int32),
            pltpu.VMEM(counts.shape, jnp.int32),
            dma((2,)),
        ],
        compiler_params=pltpu.CompilerParams(collective_id=0, has_side_effects=True, vmem_limit_bytes=25 << 20),
    )(*(pltpu.with_memory_space_constraint(a, pltpu.HBM) for a in (cols, counts, own, tiles)))


def feat_sum_kernel(share, out, held, ss, rs):
    me, size = lax.axis_index("feat"), held.shape[0]
    peers = [lax.rem(me + p, size) for p in range(1, size)]
    barrier = pltpu.get_barrier_semaphore()
    for peer in peers:
        pl.semaphore_signal(barrier, inc=1, device_id={"feat": peer}, device_id_type=MESH)
    held[me] = share[...]
    pl.semaphore_wait(barrier, size - 1)
    copies = [
        pltpu.make_async_remote_copy(
            src_ref=held.at[me],
            dst_ref=held.at[me],
            send_sem=ss.at[i],
            recv_sem=rs.at[i],
            device_id={"feat": peer},
            device_id_type=MESH,
        )
        for i, peer in enumerate(peers)
    ]
    for copy in copies:
        copy.start()
    for copy in copies:
        copy.wait()
    out[...] = sum(held[i] for i in range(size))


def feat_sum(share):
    size = lax.axis_size("feat")
    vmem = pl.BlockSpec(memory_space=pltpu.VMEM)
    return pl.pallas_call(
        feat_sum_kernel,
        out_shape=jax.ShapeDtypeStruct(share.shape, jnp.float32),
        in_specs=[vmem],
        out_specs=vmem,
        scratch_shapes=[
            pltpu.VMEM((size,) + share.shape, jnp.float32),
            pltpu.SemaphoreType.DMA((size - 1,)),
            pltpu.SemaphoreType.DMA((size - 1,)),
        ],
        compiler_params=pltpu.CompilerParams(collective_id=1, has_side_effects=True, vmem_limit_bytes=2 << 20),
    )(share)


def per_device(features, norm_gain, row_counts, tile_cols, tile_values):
    node_dev, feat_dev = features.shape
    side = tile_values.shape[1]
    blocks = node_dev // side
    total = tile_values.shape[0]
    own = features.reshape(blocks, side, feat_dev)
    *blocks_got, plan, tiles = exchange(tile_cols.reshape(1, total), row_counts, own, tile_values)
    panel, heavy = blocks_got[:PARTS], [h.reshape((blocks * HEAVY,) + h.shape[-2:]) for h in blocks_got[PARTS:]]
    aggregate = tile_product(plan, tiles, panel, heavy)
    square_sum = feat_sum(jnp.sum(aggregate * aggregate, axis=2))
    mean_square = square_sum / (feat_dev * lax.axis_size("feat"))
    normed = aggregate * norm_gain[None, None, :] * lax.rsqrt(mean_square + 1e-05)[:, :, None]
    return normed.reshape(node_dev, feat_dev)


def solution(mesh):
    placed = (P("rows", "feat"), P("feat"), P("rows", None), P("rows"), P("rows", None, None))
    return jax.shard_map(
        per_device, mesh=mesh, in_specs=placed, out_specs=P("rows", "feat"), check_vma=False
    )
```

```python
import functools

import jax
import jax.numpy as jnp
from jax import lax
from jax.experimental import pallas as pl
from jax.experimental.pallas import tpu as pltpu
from jax.sharding import PartitionSpec as P

HEAVY = 3
GROUP = 16
TOGETHER = 8


def halves(value):
    high = value.astype(jnp.bfloat16)
    return high, (value - high.astype(jnp.float32)).astype(jnp.bfloat16)


def tile_kernel(plan, tiles, *rest):
    panel, heavy = rest[:PARTS], rest[PARTS : 2 * PARTS]
    out = rest[2 * PARTS]
    total, light = tiles.shape[0], panel[0].shape[0]
    out[...] = jnp.zeros_like(out)

    def product(p, source):
        x_hi, x_lo = halves(jnp.maximum(source(plan[0, p]), 0.0))
        a = tiles[plan[2, p]]
        return jnp.dot(a, jnp.concatenate([x_hi, x_hi], axis=0), preferred_element_type=jnp.float32) + jnp.dot(
            a[:, : a.shape[1] // 2], x_lo, preferred_element_type=jnp.float32
        )

    def join(parts):
        return jnp.concatenate(list(parts), axis=0)

    def from_panel(slot):
        return join(panel[k][slot] for k in range(PARTS))

    def from_heavy(slot):
        return join(heavy[k][slot - light] for k in range(PARTS))

    def from_either(slot):
        i, j = jnp.minimum(slot, light - 1), jnp.maximum(slot - light, 0)
        return join(jnp.where(slot < light, panel[k][i], heavy[k][j]) for k in range(PARTS))

    def run(first, last, source):
        @pl.loop(first, last)
        def _(step):
            ps = [step * TOGETHER + u for u in range(TOGETHER)]
            products = [product(p, source) for p in ps]
            for p, prod in zip(ps, products):
                out[plan[1, p]] += prod

    low = lax.div(plan[3, 0], TOGETHER)
    high = lax.div(plan[3, 0] + TOGETHER - 1, TOGETHER)
    run(0, low, from_panel)
    run(low, high, from_either)
    run(high, total // TOGETHER, from_heavy)


def tile_product(plan, tiles, panel, heavy):
    side = tiles.shape[1]
    blocks, feat = panel[0].shape[0] - PLANE * PLANES, panel[0].shape[-1]
    vmem = pl.BlockSpec(memory_space=pltpu.VMEM)
    return pl.pallas_call(
        tile_kernel,
        out_shape=jax.ShapeDtypeStruct((blocks, side, feat), jnp.float32),
        in_specs=[pl.BlockSpec(memory_space=pltpu.SMEM)] + [vmem] * (2 * PARTS + 1),
        out_specs=vmem,
        compiler_params=pltpu.CompilerParams(vmem_limit_bytes=8 << 20),
    )(plan, tiles, *panel, *heavy)


PARTS = 8
PLANE = 8
PLANES = 8
ORDER = tuple((stage, stage) for stage in range(10))
MESH = pl.DeviceIdType.MESH


def total_of(mask, values, axis):
    return jnp.sum(jnp.where(mask, values, 0), axis=axis, keepdims=True)


def plan_rows(me, cols, counts, blocks):
    lanes = cols.shape[1]
    devices, shift = PLANE * PLANES, blocks.bit_length() - 1
    i = lax.broadcasted_iota(jnp.int32, (lanes, lanes), 0)
    j = lax.broadcasted_iota(jnp.int32, (lanes, lanes), 1)
    lane, down = j[:1], i[:, :1]

    def panel_slot(stripe):
        ahead = ((stripe >> 3) - me // PLANE + PLANES) & (PLANES - 1)
        return (stripe & (PLANE - 1)) * PLANES + jnp.where(ahead < 4, 2 * ahead, 2 * (PLANES - ahead) - 1)

    spread = jnp.broadcast_to(cols, (lanes, lanes))
    turned = spread.T
    hit = (turned >> shift) == j
    wanted = jnp.max(jnp.where(hit, turned & (blocks - 1), 0), axis=0, keepdims=True)
    marked = (total_of(hit, 1, 0) >= 2) & (lane != me)
    i_am_heavy = total_of(marked, 1, 1) < HEAVY
    marked = marked | ((lane == me) & i_am_heavy)
    hit_down = (spread >> shift) == i
    marked_down = (total_of(hit_down, 1, 1) >= 2) & (down != me)
    marked_down = marked_down | ((down == me) & i_am_heavy)
    rank = total_of(jnp.broadcast_to(marked_down, i.shape) & (i < j), 1, 0)
    rank_down = total_of(jnp.broadcast_to(marked, i.shape) & (j < i), 1, 1)
    request = jnp.where(marked | (lane == me), me & (GROUP - 1), wanted)
    for s in range(HEAVY):
        request = jnp.where(lane == devices + s, total_of(marked & (rank == s), panel_slot(lane), 1), request)
    heavy_hit = hit_down & marked_down
    local = cols & (blocks - 1)
    slot = jnp.where(
        total_of(heavy_hit, 1, 0) > 0,
        devices + blocks + ((local & (PLANE - 1)) * 2 + (local >> 3)) * HEAVY + total_of(heavy_hit, jnp.broadcast_to(rank_down, i.shape), 0),
        panel_slot(cols >> shift),
    )
    slot = jnp.where((cols >> shift) == me, devices + local, slot)
    side = counts.shape[1]
    ends = total_of(j[:side, :side] <= i[:side, :side], jnp.broadcast_to(counts, (side, side)), 1)
    row = total_of(ends <= j[:side], 1, 0)
    turned_slot, turned_row = [jnp.broadcast_to(v, (lanes, lanes)).T for v in (slot, row)]
    heavy_tile = slot >= devices + blocks
    light_tiles = total_of(slot < devices + blocks, 1, 1)
    place = total_of(((turned_slot >= devices + blocks) == heavy_tile) & (i < j), 1, 0) + jnp.where(heavy_tile, light_tiles, 0)
    here = jnp.broadcast_to(place, (lanes, lanes)).T == j
    ordered = [total_of(here, v, 0) for v in (turned_slot, turned_row, i)]
    return request, ordered + [jnp.broadcast_to(light_tiles, (1, lanes))]


def exchange_kernel(cols, counts, features, tiles, *rest):
    arrived, gathered = rest[:PARTS], rest[PARTS : 2 * PARTS]
    plan_out, tiles_out, scratch = rest[2 * PARTS], rest[2 * PARTS + 1], rest[2 * PARTS + 2 :]
    names = ("own", "up1", "down1", "up2", "down2", "up3s", "down3s", "up3", "down3", "far", "picked")
    bufs = {n: scratch[i * PARTS : (i + 1) * PARTS] for i, n in enumerate(names)}
    own, up1, down1, up2, down2, up3s, down3s, up3, down3, far, picked = (bufs[n] for n in names)
    (rows_buf, table, load_sem, zs, zr, xs, xr, gs, gr, out_sem, ps, pr, table_sem, staged, tile_sem, cols_buf, counts_buf, small_sem) = scratch[len(names) * PARTS :]
    me = lax.axis_index("rows")
    z, q = me // PLANE, lax.rem(me, PLANE)
    x, c = q // 2, lax.rem(q, 2)
    part_rows = own[0].shape[1]

    def at(dz):
        return lax.rem(z + dz + PLANES, PLANES)

    up, down = at(1) * PLANE + q, at(-1) * PLANE + q
    even = 1 - lax.rem(z, 2)
    partner = (z + 2 * even - 1) * PLANE + q
    right = z * PLANE + lax.rem(x + 1, 4) * 2 + c
    left = z * PLANE + lax.rem(x + 3, 4) * 2 + c
    other = z * PLANE + x * 2 + 1 - c

    def load(k):
        return pltpu.make_async_copy(features.at[:, pl.ds(k * part_rows, part_rows)], own[k], load_sem.at[k])

    for k in range(PARTS):
        load(k).start()
    small_loads = (
        pltpu.make_async_copy(cols, cols_buf, small_sem.at[0]),
        pltpu.make_async_copy(counts, counts_buf, small_sem.at[1]),
    )
    for copy in small_loads:
        copy.start()
    lot = staged.shape[1]

    def tile_load(n):
        return pltpu.make_async_copy(tiles.at[pl.ds(n * lot, lot)], staged.at[n % 2], tile_sem.at[n % 2])

    def split_tiles(n):
        tile_load(n).wait()

        @pl.loop(0, lot)
        def _(i):
            high, low = halves(staged[n % 2, i])
            tiles_out[n * lot + i] = jnp.concatenate([high, low], axis=1)

        if (n + 2) * lot < tiles.shape[0]:
            tile_load(n + 2).start()

    for n in range(2):
        tile_load(n).start()
    barrier = pltpu.get_barrier_semaphore()
    second_up, second_down = at(2) * PLANE + q, at(-2) * PLANE + q
    for peer in (up, down, second_up, second_down):
        pl.semaphore_signal(barrier, inc=1, device_id={"rows": peer}, device_id_type=MESH)

    @pl.loop(1, PLANE)
    def _(p):
        peer = z * PLANE + lax.rem(q + p, PLANE)
        pl.semaphore_signal(barrier, inc=1, device_id={"rows": peer}, device_id_type=MESH)

    pl.semaphore_wait(barrier, PLANE + 3)

    def send(src, dst, ssem, rsem, peer):
        return pltpu.make_async_remote_copy(
            src_ref=src, dst_ref=dst, send_sem=ssem, recv_sem=rsem, device_id={"rows": peer}, device_id_type=MESH
        )

    def z_copies(k, step):
        src_up, dst_up, src_down, dst_down = (
            (own[k], up1[k], own[k], down1[k]),
            (up1[k], up2[k], down1[k], down2[k]),
            (up3s[k], up3[k], down3s[k], down3[k]),
            (up3[k].at[pl.ds(PLANE, 4)], far[k].at[0], down3[k].at[pl.ds(PLANE, 4)], far[k].at[1]),
        )[step]
        i = (k * 4 + step) * 2
        return (
            send(src_up, dst_up, zs.at[k], zr.at[i], up),
            send(src_down, dst_down, zs.at[PARTS + k], zr.at[i + 1], down),
        )

    def z_start(k, step):
        for copy in z_copies(k, step):
            copy.start()

    def z_wait(k, step):
        for copy in z_copies(k, step):
            copy.wait_recv()

    def block_of(dz_reader, reader, dz_owner):
        return table[at(dz_reader) * PLANE + reader, 0, at(dz_owner) * PLANE + q]

    def plane_rows(dz):
        return pl.ds(at(dz) * PLANE, PLANE)

    def table_copy(i, dz):
        return pltpu.make_async_copy(rows_buf.at[plane_rows(dz)], table.at[plane_rows(dz)], table_sem.at[i])

    hops = ((up, -1), (down, 1), (second_up, -2), (second_down, 2))

    def rows_copy(i):
        src = rows_buf.at[plane_rows(0)]
        return send(src, src, ps.at[1 + i], pr.at[1 + i], hops[i][0])

    def share_plan():
        for copy in small_loads:
            copy.wait()
        request, plan = plan_rows(me, cols_buf[...], counts_buf[...], own[0].shape[0])
        for i, line in enumerate(plan):
            plan_out[i : i + 1] = line
        rows_buf[me] = request

        @pl.loop(1, PLANE)
        def _(p):
            src = rows_buf.at[me]
            send(src, src, ps.at[0], pr.at[0], z * PLANE + lax.rem(q + p, PLANE)).start()

        most = rows_buf.at[pl.ds(0, PLANE - 1)]
        pltpu.make_async_copy(most, most, pr.at[0]).wait()
        for i in range(4):
            rows_copy(i).start()
        table_copy(0, 0).start()
        table_copy(0, 0).wait()

    def take_plan():
        for i, (_, dz) in enumerate(hops):
            src = rows_buf.at[plane_rows(dz)]
            pltpu.make_async_copy(src, src, pr.at[1 + i]).wait()
            table_copy(1 + i, dz).start()
        for i, (_, dz) in enumerate(hops):
            table_copy(1 + i, dz).wait()

    def x_pick(k, first, sources):
        @pl.loop(0, PLANE)
        def _(reader):
            for i, (ref, dz) in enumerate(sources):
                picked[k][reader, first + i] = ref[block_of(0, reader, dz)]

        arrived[k][pl.ds(q * PLANES + first, len(sources))] = picked[k][q, pl.ds(first, len(sources))]

        @pl.loop(1, PLANE)
        def _(p):
            reader = lax.rem(q + p, PLANE)
            send(
                picked[k].at[reader, pl.ds(first, len(sources))],
                arrived[k].at[pl.ds(q * PLANES + first, len(sources))],
                xs.at[k],
                xr.at[k],
                z * PLANE + reader,
            ).start()

    def x_pass(k, first, source):
        arrived[k][q * PLANES + first] = source(q)[...]

        @pl.loop(1, PLANE)
        def _(p):
            reader = lax.rem(q + p, PLANE)
            send(source(reader), arrived[k].at[q * PLANES + first], xs.at[k], xr.at[k], z * PLANE + reader).start()

    def q_of(xx):
        return lax.rem(x + xx + 4, 4) * 2 + c

    def pieces_copy(k, i, qq, part, peer):
        piece = gathered[k].at[qq, part]
        return send(piece, piece, gs.at[k], gr.at[k * 15 + i], peer)

    def to_partner(k):
        return pieces_copy(k, 14, q, 1 - even, partner)

    def over_x(k, p):
        part = even if p else 1 - even
        return [pieces_copy(k, p * 7 + i, q, part, peer) for i, peer in enumerate((right, left))]

    def across(k, p):
        return pieces_copy(k, p * 7 + 2, q_of(1 if p else -1), even if p else 1 - even, left if p else right)

    def to_core(k, p):
        part = even if p else 1 - even
        return [pieces_copy(k, p * 7 + 3 + i, q_of(xx), part, other) for i, xx in enumerate((0, -1, 1, 2))]

    def keep_own(k):
        part = pl.ds(PLANE * PLANES, own[k].shape[0])
        return pltpu.make_async_copy(features.at[:, pl.ds(k * part_rows, part_rows)], arrived[k].at[part], out_sem.at[k])

    def z_first(k):
        load(k).wait()
        z_start(k, 0)

    def all_blocks(k, count, sem):
        whole = arrived[k].at[pl.ds(0, count)]
        pltpu.make_async_copy(whole, whole, sem).wait()

    def plan_sent():
        most = rows_buf.at[pl.ds(0, PLANE - 1)]
        pltpu.make_async_copy(most, most, ps.at[0]).wait()
        for i in range(4):
            rows_copy(i).wait_send()

    def stage(k, s):
        if s == 0:
            if k == 0:
                z_first(0)
                share_plan()
                for part in range(PARTS):
                    if part == 1:
                        z_first(1)
                    elif part:
                        load(part).wait()
                    keep_own(part).start()
                    x_pick(part, 0, [(own[part], 0)])
            elif k > 1:
                z_start(k, 0)
        elif s == 1:
            z_wait(k, 0)
            z_start(k, 1)
            x_pick(k, 1, [(up1[k], -1), (down1[k], 1)])
        elif s == 2:
            z_wait(k, 1)
            if k == 0:
                take_plan()

            @pl.loop(0, PLANE)
            def _(reader):
                up3s[k][reader] = up2[k][block_of(1, reader, -2)]
                down3s[k][reader] = down2[k][block_of(-1, reader, 2)]

            @pl.loop(0, 4)
            def _(half):
                up3s[k][PLANE + half] = up2[k][block_of(2, 2 * half, -2)]
                down3s[k][PLANE + half] = down2[k][block_of(-2, 2 * half + 1, 2)]

            z_start(k, 2)
            x_pick(k, 3, [(up2[k], -2), (down2[k], 2)])
        elif s == 3:
            z_wait(k, 2)
            z_start(k, 3)
            x_pass(k, 5, lambda reader: up3[k].at[reader])
            x_pass(k, 6, lambda reader: down3[k].at[reader])
        elif s == 4:
            z_wait(k, 3)
            x_pass(k, 7, lambda reader: far[k].at[lax.rem(reader, 2), reader // 2])
        elif s == 5:
            all_blocks(k, (PLANE - 1) * PLANES, xr.at[k])
            keep_own(k).wait()
            for i in range(HEAVY):
                gathered[k][q, 1 - even, i] = arrived[k][table[me, 0, PLANES * PLANE + i]]
            for copy in [to_partner(k)] + over_x(k, 0) + to_core(k, 0)[:1]:
                copy.start()
            if k == 0:
                plan_sent()
            for sem in (zs.at[k], zs.at[PARTS + k]):
                all_blocks(k, 2 * own[k].shape[0] + PLANE + 8, sem)
            all_blocks(k, (PLANE - 1) * PLANES, xs.at[k])
        elif s == 6:
            to_partner(k).wait_recv()
            for copy in over_x(k, 1) + to_core(k, 1)[:1]:
                copy.start()
            for came in over_x(k, 0):
                came.wait_recv()
            for copy in [across(k, 0)] + to_core(k, 0)[1:3]:
                copy.start()
        elif s == 7:
            for came in over_x(k, 1):
                came.wait_recv()
            for copy in [across(k, 1)] + to_core(k, 1)[1:3]:
                copy.start()
            across(k, 0).wait_recv()
            to_core(k, 0)[3].start()
        elif s == 8:
            across(k, 1).wait_recv()
            to_core(k, 1)[3].start()
        elif s == 9:
            for copy in to_core(k, 0) + to_core(k, 1):
                copy.wait_recv()
            all_blocks(k, 15 * HEAVY, gs.at[k])

    for t in range(PARTS + 9):
        for s, lag in ORDER:
            if 0 <= t - lag < PARTS:
                stage(t - lag, s)
        for n in (2 * t, 2 * t + 1):
            if n * lot < tiles.shape[0]:
                split_tiles(n)


def exchange(cols, counts, own, tiles):
    blocks, side, feat = own.shape
    rows = side // PARTS
    vmem = pl.BlockSpec(memory_space=pltpu.VMEM)
    hbm = pl.BlockSpec(memory_space=pltpu.HBM)
    leads = [(blocks,)] * 5 + [(PLANE + 4,)] * 4 + [(2, 4), (PLANE, 5)]
    bufs = [pltpu.VMEM(lead + (rows, feat), jnp.float32) for lead in leads for _ in range(PARTS)]
    dma = pltpu.SemaphoreType.DMA
    return pl.pallas_call(
        exchange_kernel,
        out_shape=[jax.ShapeDtypeStruct((PLANE * PLANES + blocks, rows, feat), jnp.float32)] * PARTS
        + [jax.ShapeDtypeStruct((PLANE, 2, HEAVY, rows, feat), jnp.float32)] * PARTS
        + [jax.ShapeDtypeStruct((4, cols.shape[1]), jnp.int32)]
        + [jax.ShapeDtypeStruct(tiles.shape[:2] + (2 * tiles.shape[2],), jnp.bfloat16)],
        in_specs=[hbm] * 4,
        out_specs=[vmem] * (2 * PARTS + 2),
        scratch_shapes=bufs
        + [
            pltpu.VMEM((PLANE * PLANES, 1, cols.shape[1]), jnp.int32),
            pltpu.SMEM((PLANE * PLANES, 1, cols.shape[1]), jnp.int32),
            dma((PARTS,)),
            dma((PARTS * 2,)),
            dma((PARTS * 8,)),
            dma((PARTS,)),
            dma((PARTS,)),
            dma((PARTS,)),
            dma((PARTS * 15,)),
            dma((PARTS,)),
            dma((5,)),
            dma((5,)),
            dma((5,)),
            pltpu.VMEM((2, 8) + tiles.shape[1:], jnp.float32),
            dma((2,)),
            pltpu.VMEM(cols.shape, jnp.int32),
            pltpu.VMEM(counts.shape, jnp.int32),
            dma((2,)),
        ],
        compiler_params=pltpu.CompilerParams(collective_id=0, has_side_effects=True, vmem_limit_bytes=25 << 20),
    )(*(pltpu.with_memory_space_constraint(a, pltpu.HBM) for a in (cols, counts, own, tiles)))


def feat_sum_kernel(share, out, held, ss, rs):
    me, size = lax.axis_index("feat"), held.shape[0]
    peers = [lax.rem(me + p, size) for p in range(1, size)]
    barrier = pltpu.get_barrier_semaphore()
    for peer in peers:
        pl.semaphore_signal(barrier, inc=1, device_id={"feat": peer}, device_id_type=MESH)
    held[me] = share[...]
    pl.semaphore_wait(barrier, size - 1)
    copies = [
        pltpu.make_async_remote_copy(
            src_ref=held.at[me],
            dst_ref=held.at[me],
            send_sem=ss.at[i],
            recv_sem=rs.at[i],
            device_id={"feat": peer},
            device_id_type=MESH,
        )
        for i, peer in enumerate(peers)
    ]
    for copy in copies:
        copy.start()
    for copy in copies:
        copy.wait()
    out[...] = sum(held[i] for i in range(size))


def feat_sum(share):
    size = lax.axis_size("feat")
    vmem = pl.BlockSpec(memory_space=pltpu.VMEM)
    return pl.pallas_call(
        feat_sum_kernel,
        out_shape=jax.ShapeDtypeStruct(share.shape, jnp.float32),
        in_specs=[vmem],
        out_specs=vmem,
        scratch_shapes=[
            pltpu.VMEM((size,) + share.shape, jnp.float32),
            pltpu.SemaphoreType.DMA((size - 1,)),
            pltpu.SemaphoreType.DMA((size - 1,)),
        ],
        compiler_params=pltpu.CompilerParams(collective_id=1, has_side_effects=True, vmem_limit_bytes=2 << 20),
    )(share)


def per_device(features, norm_gain, row_counts, tile_cols, tile_values):
    node_dev, feat_dev = features.shape
    side = tile_values.shape[1]
    blocks = node_dev // side
    total = tile_values.shape[0]
    own = features.reshape(blocks, side, feat_dev)
    *blocks_got, plan, tiles = exchange(tile_cols.reshape(1, total), row_counts, own, tile_values)
    panel, heavy = blocks_got[:PARTS], [h.reshape((blocks * HEAVY,) + h.shape[-2:]) for h in blocks_got[PARTS:]]
    aggregate = tile_product(plan, tiles, panel, heavy)
    square_sum = feat_sum(jnp.sum(aggregate * aggregate, axis=2))
    mean_square = square_sum / (feat_dev * lax.axis_size("feat"))
    normed = aggregate * norm_gain[None, None, :] * lax.rsqrt(mean_square + 1e-05)[:, :, None]
    return normed.reshape(node_dev, feat_dev)


def solution(mesh):
    placed = (P("rows", "feat"), P("feat"), P("rows", None), P("rows"), P("rows", None, None))
    return jax.shard_map(
        per_device, mesh=mesh, in_specs=placed, out_specs=P("rows", "feat"), check_vma=False
    )
```

```python
import functools

import jax
import jax.numpy as jnp
from jax import lax
from jax.experimental import pallas as pl
from jax.experimental.pallas import tpu as pltpu
from jax.sharding import PartitionSpec as P

HEAVY = 3
GROUP = 16
TOGETHER = 16


def halves(value):
    high = value.astype(jnp.bfloat16)
    return high, (value - high.astype(jnp.float32)).astype(jnp.bfloat16)


def tile_kernel(plan, tiles, *rest):
    panel, heavy = rest[:PARTS], rest[PARTS : 2 * PARTS]
    out = rest[2 * PARTS]
    total, light = tiles.shape[0], panel[0].shape[0]
    out[...] = jnp.zeros_like(out)

    def product(p, source):
        x_hi, x_lo = halves(jnp.maximum(source(plan[0, p]), 0.0))
        a = tiles[plan[2, p]]
        return jnp.dot(a, jnp.concatenate([x_hi, x_hi], axis=0), preferred_element_type=jnp.float32) + jnp.dot(
            a[:, : a.shape[1] // 2], x_lo, preferred_element_type=jnp.float32
        )

    def join(parts):
        return jnp.concatenate(list(parts), axis=0)

    def from_panel(slot):
        return join(panel[k][slot] for k in range(PARTS))

    def from_heavy(slot):
        return join(heavy[k][slot - light] for k in range(PARTS))

    def from_either(slot):
        i, j = jnp.minimum(slot, light - 1), jnp.maximum(slot - light, 0)
        return join(jnp.where(slot < light, panel[k][i], heavy[k][j]) for k in range(PARTS))

    def run(first, last, source):
        @pl.loop(first, last)
        def _(step):
            ps = [step * TOGETHER + u for u in range(TOGETHER)]
            products = [product(p, source) for p in ps]
            for p, prod in zip(ps, products):
                out[plan[1, p]] += prod

    low = lax.div(plan[3, 0], TOGETHER)
    high = lax.div(plan[3, 0] + TOGETHER - 1, TOGETHER)
    run(0, low, from_panel)
    run(low, high, from_either)
    run(high, total // TOGETHER, from_heavy)


def tile_product(plan, tiles, panel, heavy):
    side = tiles.shape[1]
    blocks, feat = panel[0].shape[0] - PLANE * PLANES, panel[0].shape[-1]
    vmem = pl.BlockSpec(memory_space=pltpu.VMEM)
    return pl.pallas_call(
        tile_kernel,
        out_shape=jax.ShapeDtypeStruct((blocks, side, feat), jnp.float32),
        in_specs=[pl.BlockSpec(memory_space=pltpu.SMEM)] + [vmem] * (2 * PARTS + 1),
        out_specs=vmem,
        compiler_params=pltpu.CompilerParams(vmem_limit_bytes=8 << 20),
    )(plan, tiles, *panel, *heavy)


PARTS = 8
PLANE = 8
PLANES = 8
STRAIGHT = 1
ORDER = tuple((stage, stage) for stage in range(10))
MESH = pl.DeviceIdType.MESH


def total_of(mask, values, axis):
    return jnp.sum(jnp.where(mask, values, 0), axis=axis, keepdims=True)


def plan_rows(me, cols, counts, blocks):
    lanes = cols.shape[1]
    devices, shift = PLANE * PLANES, blocks.bit_length() - 1
    i = lax.broadcasted_iota(jnp.int32, (lanes, lanes), 0)
    j = lax.broadcasted_iota(jnp.int32, (lanes, lanes), 1)
    lane, down = j[:1], i[:, :1]

    def panel_slot(stripe):
        ahead = ((stripe >> 3) - me // PLANE + PLANES) & (PLANES - 1)
        return (stripe & (PLANE - 1)) * PLANES + jnp.where(ahead < 4, 2 * ahead, 2 * (PLANES - ahead) - 1)

    spread = jnp.broadcast_to(cols, (lanes, lanes))
    turned = spread.T
    hit = (turned >> shift) == j
    wanted = jnp.max(jnp.where(hit, turned & (blocks - 1), 0), axis=0, keepdims=True)
    marked = (total_of(hit, 1, 0) >= 2) & (lane != me)
    i_am_heavy = total_of(marked, 1, 1) < HEAVY
    marked = marked | ((lane == me) & i_am_heavy)
    hit_down = (spread >> shift) == i
    marked_down = (total_of(hit_down, 1, 1) >= 2) & (down != me)
    marked_down = marked_down | ((down == me) & i_am_heavy)
    rank = total_of(jnp.broadcast_to(marked_down, i.shape) & (i < j), 1, 0)
    rank_down = total_of(jnp.broadcast_to(marked, i.shape) & (j < i), 1, 1)
    request = jnp.where(marked | (lane == me), me & (GROUP - 1), wanted)
    for s in range(HEAVY):
        request = jnp.where(lane == devices + s, total_of(marked & (rank == s), panel_slot(lane), 1), request)
    heavy_hit = hit_down & marked_down
    local = cols & (blocks - 1)
    slot = jnp.where(
        total_of(heavy_hit, 1, 0) > 0,
        devices + blocks + ((local & (PLANE - 1)) * 2 + (local >> 3)) * HEAVY + total_of(heavy_hit, jnp.broadcast_to(rank_down, i.shape), 0),
        panel_slot(cols >> shift),
    )
    slot = jnp.where((cols >> shift) == me, devices + local, slot)
    side = counts.shape[1]
    ends = total_of(j[:side, :side] <= i[:side, :side], jnp.broadcast_to(counts, (side, side)), 1)
    row = total_of(ends <= j[:side], 1, 0)
    turned_slot, turned_row = [jnp.broadcast_to(v, (lanes, lanes)).T for v in (slot, row)]
    heavy_tile = slot >= devices + blocks
    light_tiles = total_of(slot < devices + blocks, 1, 1)
    place = total_of(((turned_slot >= devices + blocks) == heavy_tile) & (i < j), 1, 0) + jnp.where(heavy_tile, light_tiles, 0)
    here = jnp.broadcast_to(place, (lanes, lanes)).T == j
    ordered = [total_of(here, v, 0) for v in (turned_slot, turned_row, i)]
    return request, ordered + [jnp.broadcast_to(light_tiles, (1, lanes))]


def exchange_kernel(cols, counts, features, tiles, *rest):
    arrived, gathered = rest[:PARTS], rest[PARTS : 2 * PARTS]
    plan_out, tiles_out, scratch = rest[2 * PARTS], rest[2 * PARTS + 1], rest[2 * PARTS + 2 :]
    names = ("own", "up1", "down1", "up2", "down2", "up3s", "down3s", "up3", "down3", "far", "picked")
    bufs = {n: scratch[i * PARTS : (i + 1) * PARTS] for i, n in enumerate(names)}
    own, up1, down1, up2, down2, up3s, down3s, up3, down3, far, picked = (bufs[n] for n in names)
    (rows_buf, table, load_sem, zs, zr, xs, xr, gs, gr, out_sem, ps, pr, table_sem, staged, tile_sem, cols_buf, counts_buf, small_sem) = scratch[len(names) * PARTS :]
    me = lax.axis_index("rows")
    z, q = me // PLANE, lax.rem(me, PLANE)
    x, c = q // 2, lax.rem(q, 2)
    part_rows = own[0].shape[1]

    def at(dz):
        return lax.rem(z + dz + PLANES, PLANES)

    up, down = at(1) * PLANE + q, at(-1) * PLANE + q
    even = 1 - lax.rem(z, 2)
    right = z * PLANE + lax.rem(x + 1, 4) * 2 + c
    left = z * PLANE + lax.rem(x + 3, 4) * 2 + c
    opposite = z * PLANE + lax.rem(x + 2, 4) * 2 + c
    other = z * PLANE + x * 2 + 1 - c

    def load(k):
        return pltpu.make_async_copy(features.at[:, pl.ds(k * part_rows, part_rows)], own[k], load_sem.at[k])

    for k in range(PARTS):
        load(k).start()
    small_loads = (
        pltpu.make_async_copy(cols, cols_buf, small_sem.at[0]),
        pltpu.make_async_copy(counts, counts_buf, small_sem.at[1]),
    )
    for copy in small_loads:
        copy.start()
    lot = staged.shape[1]

    def tile_load(n):
        return pltpu.make_async_copy(tiles.at[pl.ds(n * lot, lot)], staged.at[n % 2], tile_sem.at[n % 2])

    def split_tiles(n):
        tile_load(n).wait()

        @pl.loop(0, lot)
        def _(i):
            high, low = halves(staged[n % 2, i])
            tiles_out[n * lot + i] = jnp.concatenate([high, low], axis=1)

        if (n + 2) * lot < tiles.shape[0]:
            tile_load(n + 2).start()

    for n in range(2):
        tile_load(n).start()
    barrier = pltpu.get_barrier_semaphore()
    second_up, second_down = at(2) * PLANE + q, at(-2) * PLANE + q
    for peer in (up, down, second_up, second_down):
        pl.semaphore_signal(barrier, inc=1, device_id={"rows": peer}, device_id_type=MESH)

    @pl.loop(1, PLANE)
    def _(p):
        peer = z * PLANE + lax.rem(q + p, PLANE)
        pl.semaphore_signal(barrier, inc=1, device_id={"rows": peer}, device_id_type=MESH)

    pl.semaphore_wait(barrier, PLANE + 3)

    def send(src, dst, ssem, rsem, peer):
        return pltpu.make_async_remote_copy(
            src_ref=src, dst_ref=dst, send_sem=ssem, recv_sem=rsem, device_id={"rows": peer}, device_id_type=MESH
        )

    def z_copies(k, step):
        src_up, dst_up, src_down, dst_down = (
            (own[k], up1[k], own[k], down1[k]),
            (up1[k], up2[k], down1[k], down2[k]),
            (up3s[k], up3[k], down3s[k], down3[k]),
            (up3[k].at[pl.ds(PLANE, 4)], far[k].at[0], down3[k].at[pl.ds(PLANE, 4)], far[k].at[1]),
        )[step]
        i = (k * 4 + step) * 2
        return (
            send(src_up, dst_up, zs.at[k], zr.at[i], up),
            send(src_down, dst_down, zs.at[PARTS + k], zr.at[i + 1], down),
        )

    def z_start(k, step):
        for copy in z_copies(k, step):
            copy.start()

    def z_wait(k, step):
        for copy in z_copies(k, step):
            copy.wait_recv()

    def block_of(dz_reader, reader, dz_owner):
        return table[at(dz_reader) * PLANE + reader, 0, at(dz_owner) * PLANE + q]

    def plane_rows(dz):
        return pl.ds(at(dz) * PLANE, PLANE)

    def table_copy(i, dz):
        return pltpu.make_async_copy(rows_buf.at[plane_rows(dz)], table.at[plane_rows(dz)], table_sem.at[i])

    hops = ((up, -1), (down, 1), (second_up, -2), (second_down, 2))

    def rows_copy(i):
        src = rows_buf.at[plane_rows(0)]
        return send(src, src, ps.at[1 + i], pr.at[1 + i], hops[i][0])

    def share_plan():
        for copy in small_loads:
            copy.wait()
        request, plan = plan_rows(me, cols_buf[...], counts_buf[...], own[0].shape[0])
        for i, line in enumerate(plan):
            plan_out[i : i + 1] = line
        rows_buf[me] = request

        @pl.loop(1, PLANE)
        def _(p):
            src = rows_buf.at[me]
            send(src, src, ps.at[0], pr.at[0], z * PLANE + lax.rem(q + p, PLANE)).start()

        most = rows_buf.at[pl.ds(0, PLANE - 1)]
        pltpu.make_async_copy(most, most, pr.at[0]).wait()
        for i in range(4):
            rows_copy(i).start()
        table_copy(0, 0).start()
        table_copy(0, 0).wait()

    def take_plan():
        for i, (_, dz) in enumerate(hops):
            src = rows_buf.at[plane_rows(dz)]
            pltpu.make_async_copy(src, src, pr.at[1 + i]).wait()
            table_copy(1 + i, dz).start()
        for i, (_, dz) in enumerate(hops):
            table_copy(1 + i, dz).wait()

    def x_pick(k, first, sources):
        @pl.loop(0, PLANE)
        def _(reader):
            for i, (ref, dz) in enumerate(sources):
                picked[k][reader, first + i] = ref[block_of(0, reader, dz)]

        arrived[k][pl.ds(q * PLANES + first, len(sources))] = picked[k][q, pl.ds(first, len(sources))]

        @pl.loop(1, PLANE)
        def _(p):
            reader = lax.rem(q + p, PLANE)
            send(
                picked[k].at[reader, pl.ds(first, len(sources))],
                arrived[k].at[pl.ds(q * PLANES + first, len(sources))],
                xs.at[k],
                xr.at[k],
                z * PLANE + reader,
            ).start()

    def x_pass(k, first, source):
        arrived[k][q * PLANES + first] = source(q)[...]

        @pl.loop(1, PLANE)
        def _(p):
            reader = lax.rem(q + p, PLANE)
            send(source(reader), arrived[k].at[q * PLANES + first], xs.at[k], xr.at[k], z * PLANE + reader).start()

    def q_of(xx):
        return lax.rem(x + xx + 4, 4) * 2 + c

    def pieces_copy(k, i, qq, part, peer):
        piece = gathered[k].at[qq, part]
        return send(piece, piece, gs.at[k], gr.at[k * 15 + i], peer)

    def to_partner(k):
        return pieces_copy(k, 14, q, 1 - even, jnp.where(even == k % 2, up, down))

    def over_x(k, p):
        part = even if p else 1 - even
        return [pieces_copy(k, p * 7 + i, q, part, peer) for i, peer in enumerate((right, left))]

    def direct(k):
        return k >= PARTS - STRAIGHT

    def across(k, p):
        part, i = even if p else 1 - even, p * 7 + 2
        if direct(k):
            return pieces_copy(k, i, q, part, opposite)
        return pieces_copy(k, i, q_of(1 if p else -1), part, left if p else right)

    def to_core(k, p):
        part = even if p else 1 - even
        return [pieces_copy(k, p * 7 + 3 + i, q_of(xx), part, other) for i, xx in enumerate((0, -1, 1, 2))]

    def keep_own(k):
        part = pl.ds(PLANE * PLANES, own[k].shape[0])
        return pltpu.make_async_copy(features.at[:, pl.ds(k * part_rows, part_rows)], arrived[k].at[part], out_sem.at[k])

    def z_first(k):
        load(k).wait()
        z_start(k, 0)

    def all_blocks(k, count, sem):
        whole = arrived[k].at[pl.ds(0, count)]
        pltpu.make_async_copy(whole, whole, sem).wait()

    def plan_sent():
        most = rows_buf.at[pl.ds(0, PLANE - 1)]
        pltpu.make_async_copy(most, most, ps.at[0]).wait()
        for i in range(4):
            rows_copy(i).wait_send()

    def stage(k, s):
        if s == 0:
            if k == 0:
                z_first(0)
                share_plan()
                for part in range(PARTS):
                    if part == 1:
                        z_first(1)
                    elif part:
                        load(part).wait()
                    keep_own(part).start()
                    x_pick(part, 0, [(own[part], 0)])
            elif k > 1:
                z_start(k, 0)
        elif s == 1:
            z_wait(k, 0)
            z_start(k, 1)
            x_pick(k, 1, [(up1[k], -1), (down1[k], 1)])
        elif s == 2:
            z_wait(k, 1)
            if k == 0:
                take_plan()

            @pl.loop(0, PLANE)
            def _(reader):
                up3s[k][reader] = up2[k][block_of(1, reader, -2)]
                down3s[k][reader] = down2[k][block_of(-1, reader, 2)]

            @pl.loop(0, 4)
            def _(half):
                up3s[k][PLANE + half] = up2[k][block_of(2, 2 * half, -2)]
                down3s[k][PLANE + half] = down2[k][block_of(-2, 2 * half + 1, 2)]

            z_start(k, 2)
            x_pick(k, 3, [(up2[k], -2), (down2[k], 2)])
        elif s == 3:
            z_wait(k, 2)
            z_start(k, 3)
            x_pass(k, 5, lambda reader: up3[k].at[reader])
            x_pass(k, 6, lambda reader: down3[k].at[reader])
        elif s == 4:
            z_wait(k, 3)
            x_pass(k, 7, lambda reader: far[k].at[lax.rem(reader, 2), reader // 2])
        elif s == 5:
            all_blocks(k, (PLANE - 1) * PLANES, xr.at[k])
            keep_own(k).wait()
            for i in range(HEAVY):
                gathered[k][q, 1 - even, i] = arrived[k][table[me, 0, PLANES * PLANE + i]]
            for copy in [to_partner(k)] + over_x(k, 0) + [across(k, 0)] * direct(k) + to_core(k, 0)[:1]:
                copy.start()
            if k == 0:
                plan_sent()
            for sem in (zs.at[k], zs.at[PARTS + k]):
                all_blocks(k, 2 * own[k].shape[0] + PLANE + 8, sem)
            all_blocks(k, (PLANE - 1) * PLANES, xs.at[k])
        elif s == 6:
            to_partner(k).wait_recv()
            for copy in over_x(k, 1) + [across(k, 1)] * direct(k) + to_core(k, 1)[:1]:
                copy.start()
            for came in over_x(k, 0):
                came.wait_recv()
            for copy in [across(k, 0)] * (not direct(k)) + to_core(k, 0)[1:3]:
                copy.start()
        elif s == 7:
            for came in over_x(k, 1):
                came.wait_recv()
            for copy in [across(k, 1)] * (not direct(k)) + to_core(k, 1)[1:3]:
                copy.start()
            across(k, 0).wait_recv()
            to_core(k, 0)[3].start()
        elif s == 8:
            across(k, 1).wait_recv()
            to_core(k, 1)[3].start()
        elif s == 9:
            for copy in to_core(k, 0) + to_core(k, 1):
                copy.wait_recv()
            all_blocks(k, 15 * HEAVY, gs.at[k])

    for t in range(PARTS + 9):
        for s, lag in ORDER:
            if 0 <= t - lag < PARTS:
                stage(t - lag, s)
        for n in (2 * t, 2 * t + 1):
            if n * lot < tiles.shape[0]:
                split_tiles(n)


def exchange(cols, counts, own, tiles):
    blocks, side, feat = own.shape
    rows = side // PARTS
    vmem = pl.BlockSpec(memory_space=pltpu.VMEM)
    hbm = pl.BlockSpec(memory_space=pltpu.HBM)
    leads = [(blocks,)] * 5 + [(PLANE + 4,)] * 4 + [(2, 4), (PLANE, 5)]
    bufs = [pltpu.VMEM(lead + (rows, feat), jnp.float32) for lead in leads for _ in range(PARTS)]
    dma = pltpu.SemaphoreType.DMA
    return pl.pallas_call(
        exchange_kernel,
        out_shape=[jax.ShapeDtypeStruct((PLANE * PLANES + blocks, rows, feat), jnp.float32)] * PARTS
        + [jax.ShapeDtypeStruct((PLANE, 2, HEAVY, rows, feat), jnp.float32)] * PARTS
        + [jax.ShapeDtypeStruct((4, cols.shape[1]), jnp.int32)]
        + [jax.ShapeDtypeStruct(tiles.shape[:2] + (2 * tiles.shape[2],), jnp.bfloat16)],
        in_specs=[hbm] * 4,
        out_specs=[vmem] * (2 * PARTS + 2),
        scratch_shapes=bufs
        + [
            pltpu.VMEM((PLANE * PLANES, 1, cols.shape[1]), jnp.int32),
            pltpu.SMEM((PLANE * PLANES, 1, cols.shape[1]), jnp.int32),
            dma((PARTS,)),
            dma((PARTS * 2,)),
            dma((PARTS * 8,)),
            dma((PARTS,)),
            dma((PARTS,)),
            dma((PARTS,)),
            dma((PARTS * 15,)),
            dma((PARTS,)),
            dma((5,)),
            dma((5,)),
            dma((5,)),
            pltpu.VMEM((2, 8) + tiles.shape[1:], jnp.float32),
            dma((2,)),
            pltpu.VMEM(cols.shape, jnp.int32),
            pltpu.VMEM(counts.shape, jnp.int32),
            dma((2,)),
        ],
        compiler_params=pltpu.CompilerParams(collective_id=0, has_side_effects=True, vmem_limit_bytes=25 << 20),
    )(*(pltpu.with_memory_space_constraint(a, pltpu.HBM) for a in (cols, counts, own, tiles)))


def feat_sum_kernel(share, out, held, ss, rs):
    me, size = lax.axis_index("feat"), held.shape[0]
    peers = [lax.rem(me + p, size) for p in range(1, size)]
    barrier = pltpu.get_barrier_semaphore()
    for peer in peers:
        pl.semaphore_signal(barrier, inc=1, device_id={"feat": peer}, device_id_type=MESH)
    held[me] = share[...]
    pl.semaphore_wait(barrier, size - 1)
    copies = [
        pltpu.make_async_remote_copy(
            src_ref=held.at[me],
            dst_ref=held.at[me],
            send_sem=ss.at[i],
            recv_sem=rs.at[i],
            device_id={"feat": peer},
            device_id_type=MESH,
        )
        for i, peer in enumerate(peers)
    ]
    for copy in copies:
        copy.start()
    for copy in copies:
        copy.wait()
    out[...] = sum(held[i] for i in range(size))


def feat_sum(share):
    size = lax.axis_size("feat")
    vmem = pl.BlockSpec(memory_space=pltpu.VMEM)
    return pl.pallas_call(
        feat_sum_kernel,
        out_shape=jax.ShapeDtypeStruct(share.shape, jnp.float32),
        in_specs=[vmem],
        out_specs=vmem,
        scratch_shapes=[
            pltpu.VMEM((size,) + share.shape, jnp.float32),
            pltpu.SemaphoreType.DMA((size - 1,)),
            pltpu.SemaphoreType.DMA((size - 1,)),
        ],
        compiler_params=pltpu.CompilerParams(collective_id=1, has_side_effects=True, vmem_limit_bytes=2 << 20),
    )(share)


def per_device(features, norm_gain, row_counts, tile_cols, tile_values):
    node_dev, feat_dev = features.shape
    side = tile_values.shape[1]
    blocks = node_dev // side
    total = tile_values.shape[0]
    own = features.reshape(blocks, side, feat_dev)
    *blocks_got, plan, tiles = exchange(tile_cols.reshape(1, total), row_counts, own, tile_values)
    panel, heavy = blocks_got[:PARTS], [h.reshape((blocks * HEAVY,) + h.shape[-2:]) for h in blocks_got[PARTS:]]
    aggregate = tile_product(plan, tiles, panel, heavy)
    square_sum = feat_sum(jnp.sum(aggregate * aggregate, axis=2))
    mean_square = square_sum / (feat_dev * lax.axis_size("feat"))
    normed = aggregate * norm_gain[None, None, :] * lax.rsqrt(mean_square + 1e-05)[:, :, None]
    return normed.reshape(node_dev, feat_dev)


def solution(mesh):
    placed = (P("rows", "feat"), P("feat"), P("rows", None), P("rows"), P("rows", None, None))
    return jax.shard_map(
        per_device, mesh=mesh, in_specs=placed, out_specs=P("rows", "feat"), check_vma=False
    )
```

```python
import functools

import jax
import jax.numpy as jnp
from jax import lax
from jax.experimental import pallas as pl
from jax.experimental.pallas import tpu as pltpu
from jax.sharding import PartitionSpec as P

HEAVY = 3
GROUP = 16
TOGETHER = 16


def halves(value):
    high = value.astype(jnp.bfloat16)
    return high, (value - high.astype(jnp.float32)).astype(jnp.bfloat16)


def tile_kernel(plan, tiles, *rest):
    panel, heavy = rest[:PARTS], rest[PARTS : 2 * PARTS]
    out = rest[2 * PARTS]
    total, light = tiles.shape[0], panel[0].shape[0]
    out[...] = jnp.zeros_like(out)

    def product(p, source):
        x_hi, x_lo = halves(jnp.maximum(source(plan[0, p]), 0.0))
        a = tiles[plan[2, p]]
        return jnp.dot(a, jnp.concatenate([x_hi, x_hi], axis=0), preferred_element_type=jnp.float32) + jnp.dot(
            a[:, : a.shape[1] // 2], x_lo, preferred_element_type=jnp.float32
        )

    def join(parts):
        return jnp.concatenate(list(parts), axis=0)

    def from_panel(slot):
        return join(panel[k][slot] for k in range(PARTS))

    def from_heavy(slot):
        return join(heavy[k][slot - light] for k in range(PARTS))

    def from_either(slot):
        i, j = jnp.minimum(slot, light - 1), jnp.maximum(slot - light, 0)
        return join(jnp.where(slot < light, panel[k][i], heavy[k][j]) for k in range(PARTS))

    def run(first, last, source):
        @pl.loop(first, last)
        def _(step):
            ps = [step * TOGETHER + u for u in range(TOGETHER)]
            products = [product(p, source) for p in ps]
            for p, prod in zip(ps, products):
                out[plan[1, p]] += prod

    low = lax.div(plan[3, 0], TOGETHER)
    high = lax.div(plan[3, 0] + TOGETHER - 1, TOGETHER)
    run(0, low, from_panel)
    run(low, high, from_either)
    run(high, total // TOGETHER, from_heavy)


def tile_product(plan, tiles, panel, heavy):
    side = tiles.shape[1]
    blocks, feat = panel[0].shape[0] - PLANE * PLANES, panel[0].shape[-1]
    vmem = pl.BlockSpec(memory_space=pltpu.VMEM)
    return pl.pallas_call(
        tile_kernel,
        out_shape=jax.ShapeDtypeStruct((blocks, side, feat), jnp.float32),
        in_specs=[pl.BlockSpec(memory_space=pltpu.SMEM)] + [vmem] * (2 * PARTS + 1),
        out_specs=vmem,
        compiler_params=pltpu.CompilerParams(vmem_limit_bytes=8 << 20),
    )(plan, tiles, *panel, *heavy)


PARTS = 8
PLANE = 8
PLANES = 8
STRAIGHT = 1
ORDER = tuple((stage, stage) for stage in range(10))
MESH = pl.DeviceIdType.MESH


def total_of(mask, values, axis):
    return jnp.sum(jnp.where(mask, values, 0), axis=axis, keepdims=True)


def plan_rows(me, cols, counts, blocks):
    lanes = cols.shape[1]
    devices, shift = PLANE * PLANES, blocks.bit_length() - 1
    i = lax.broadcasted_iota(jnp.int32, (lanes, lanes), 0)
    j = lax.broadcasted_iota(jnp.int32, (lanes, lanes), 1)
    lane, down = j[:1], i[:, :1]

    def panel_slot(stripe):
        ahead = ((stripe >> 3) - me // PLANE + PLANES) & (PLANES - 1)
        return (stripe & (PLANE - 1)) * PLANES + jnp.where(ahead < 4, 2 * ahead, 2 * (PLANES - ahead) - 1)

    spread = jnp.broadcast_to(cols, (lanes, lanes))
    turned = spread.T
    hit = (turned >> shift) == j
    wanted = jnp.max(jnp.where(hit, turned & (blocks - 1), 0), axis=0, keepdims=True)
    marked = (total_of(hit, 1, 0) >= 2) & (lane != me)
    i_am_heavy = total_of(marked, 1, 1) < HEAVY
    marked = marked | ((lane == me) & i_am_heavy)
    hit_down = (spread >> shift) == i
    marked_down = (total_of(hit_down, 1, 1) >= 2) & (down != me)
    marked_down = marked_down | ((down == me) & i_am_heavy)
    rank = total_of(jnp.broadcast_to(marked_down, i.shape) & (i < j), 1, 0)
    rank_down = total_of(jnp.broadcast_to(marked, i.shape) & (j < i), 1, 1)
    request = jnp.where(marked | (lane == me), me & (GROUP - 1), wanted)
    for s in range(HEAVY):
        request = jnp.where(lane == devices + s, total_of(marked & (rank == s), panel_slot(lane), 1), request)
    heavy_hit = hit_down & marked_down
    local = cols & (blocks - 1)
    slot = jnp.where(
        total_of(heavy_hit, 1, 0) > 0,
        devices + blocks + ((local & (PLANE - 1)) * 2 + (local >> 3)) * HEAVY + total_of(heavy_hit, jnp.broadcast_to(rank_down, i.shape), 0),
        panel_slot(cols >> shift),
    )
    slot = jnp.where((cols >> shift) == me, devices + local, slot)
    side = counts.shape[1]
    ends = total_of(j[:side, :side] <= i[:side, :side], jnp.broadcast_to(counts, (side, side)), 1)
    row = total_of(ends <= j[:side], 1, 0)
    turned_slot, turned_row = [jnp.broadcast_to(v, (lanes, lanes)).T for v in (slot, row)]
    heavy_tile = slot >= devices + blocks
    light_tiles = total_of(slot < devices + blocks, 1, 1)
    place = total_of(((turned_slot >= devices + blocks) == heavy_tile) & (i < j), 1, 0) + jnp.where(heavy_tile, light_tiles, 0)
    here = jnp.broadcast_to(place, (lanes, lanes)).T == j
    ordered = [total_of(here, v, 0) for v in (turned_slot, turned_row, i)]
    return request, ordered + [jnp.broadcast_to(light_tiles, (1, lanes))]


def exchange_kernel(cols, counts, features, tiles, *rest):
    arrived, gathered = rest[:PARTS], rest[PARTS : 2 * PARTS]
    plan_out, tiles_out, scratch = rest[2 * PARTS], rest[2 * PARTS + 1], rest[2 * PARTS + 2 :]
    names = ("own", "up1", "down1", "up2", "down2", "up3s", "down3s", "up3", "down3", "far", "picked")
    bufs = {n: scratch[i * PARTS : (i + 1) * PARTS] for i, n in enumerate(names)}
    own, up1, down1, up2, down2, up3s, down3s, up3, down3, far, picked = (bufs[n] for n in names)
    (rows_buf, table, load_sem, zs, zr, xs, xr, gs, gr, out_sem, ps, pr, table_sem, staged, tile_sem, cols_buf, counts_buf, small_sem) = scratch[len(names) * PARTS :]
    me = lax.axis_index("rows")
    z, q = me // PLANE, lax.rem(me, PLANE)
    x, c = q // 2, lax.rem(q, 2)
    part_rows = own[0].shape[1]

    def at(dz):
        return lax.rem(z + dz + PLANES, PLANES)

    up, down = at(1) * PLANE + q, at(-1) * PLANE + q
    even = 1 - lax.rem(z, 2)
    right = z * PLANE + lax.rem(x + 1, 4) * 2 + c
    left = z * PLANE + lax.rem(x + 3, 4) * 2 + c
    opposite = z * PLANE + lax.rem(x + 2, 4) * 2 + c
    other = z * PLANE + x * 2 + 1 - c

    def load(k):
        return pltpu.make_async_copy(features.at[:, pl.ds(k * part_rows, part_rows)], own[k], load_sem.at[k])

    for k in range(PARTS):
        load(k).start()
    small_loads = (
        pltpu.make_async_copy(cols, cols_buf, small_sem.at[0]),
        pltpu.make_async_copy(counts, counts_buf, small_sem.at[1]),
    )
    for copy in small_loads:
        copy.start()
    lot = staged.shape[1]

    def tile_load(n):
        return pltpu.make_async_copy(tiles.at[pl.ds(n * lot, lot)], staged.at[n % 2], tile_sem.at[n % 2])

    def split_tiles(n):
        tile_load(n).wait()

        @pl.loop(0, lot)
        def _(i):
            high, low = halves(staged[n % 2, i])
            tiles_out[n * lot + i] = jnp.concatenate([high, low], axis=1)

        if (n + 2) * lot < tiles.shape[0]:
            tile_load(n + 2).start()

    for n in range(2):
        tile_load(n).start()
    barrier = pltpu.get_barrier_semaphore()
    second_up, second_down = at(2) * PLANE + q, at(-2) * PLANE + q
    for peer in (up, down, second_up, second_down):
        pl.semaphore_signal(barrier, inc=1, device_id={"rows": peer}, device_id_type=MESH)

    @pl.loop(1, PLANE)
    def _(p):
        peer = z * PLANE + lax.rem(q + p, PLANE)
        pl.semaphore_signal(barrier, inc=1, device_id={"rows": peer}, device_id_type=MESH)

    pl.semaphore_wait(barrier, PLANE + 3)

    def send(src, dst, ssem, rsem, peer):
        return pltpu.make_async_remote_copy(
            src_ref=src, dst_ref=dst, send_sem=ssem, recv_sem=rsem, device_id={"rows": peer}, device_id_type=MESH
        )

    def z_copies(k, step):
        src_up, dst_up, src_down, dst_down = (
            (own[k], up1[k], own[k], down1[k]),
            (up1[k], up2[k], down1[k], down2[k]),
            (up3s[k], up3[k], down3s[k], down3[k]),
            (up3[k].at[pl.ds(PLANE, 4)], far[k].at[0], down3[k].at[pl.ds(PLANE, 4)], far[k].at[1]),
        )[step]
        i = (k * 4 + step) * 2
        return (
            send(src_up, dst_up, zs.at[k], zr.at[i], up),
            send(src_down, dst_down, zs.at[PARTS + k], zr.at[i + 1], down),
        )

    def z_start(k, step):
        for copy in z_copies(k, step):
            copy.start()

    def z_wait(k, step):
        for copy in z_copies(k, step):
            copy.wait_recv()

    def block_of(dz_reader, reader, dz_owner):
        return table[at(dz_reader) * PLANE + reader, 0, at(dz_owner) * PLANE + q]

    def plane_rows(dz):
        return pl.ds(at(dz) * PLANE, PLANE)

    def table_copy(i, dz):
        return pltpu.make_async_copy(rows_buf.at[plane_rows(dz)], table.at[plane_rows(dz)], table_sem.at[i])

    hops = ((up, -1), (down, 1), (second_up, -2), (second_down, 2))

    def rows_copy(i):
        src = rows_buf.at[plane_rows(0)]
        return send(src, src, ps.at[1 + i], pr.at[1 + i], hops[i][0])

    def share_plan():
        for copy in small_loads:
            copy.wait()
        request, plan = plan_rows(me, cols_buf[...], counts_buf[...], own[0].shape[0])
        for i, line in enumerate(plan):
            plan_out[i : i + 1] = line
        rows_buf[me] = request

        @pl.loop(1, PLANE)
        def _(p):
            src = rows_buf.at[me]
            send(src, src, ps.at[0], pr.at[0], z * PLANE + lax.rem(q + p, PLANE)).start()

        most = rows_buf.at[pl.ds(0, PLANE - 1)]
        pltpu.make_async_copy(most, most, pr.at[0]).wait()
        for i in range(4):
            rows_copy(i).start()
        table_copy(0, 0).start()
        table_copy(0, 0).wait()

    def take_plan():
        for i, (_, dz) in enumerate(hops):
            src = rows_buf.at[plane_rows(dz)]
            pltpu.make_async_copy(src, src, pr.at[1 + i]).wait()
            table_copy(1 + i, dz).start()
        for i, (_, dz) in enumerate(hops):
            table_copy(1 + i, dz).wait()

    def x_pick(k, first, sources):
        @pl.loop(0, PLANE)
        def _(reader):
            for i, (ref, dz) in enumerate(sources):
                picked[k][reader, first + i] = ref[block_of(0, reader, dz)]

        arrived[k][pl.ds(q * PLANES + first, len(sources))] = picked[k][q, pl.ds(first, len(sources))]

        @pl.loop(1, PLANE)
        def _(p):
            reader = lax.rem(q + p, PLANE)
            send(
                picked[k].at[reader, pl.ds(first, len(sources))],
                arrived[k].at[pl.ds(q * PLANES + first, len(sources))],
                xs.at[k],
                xr.at[k],
                z * PLANE + reader,
            ).start()

    def x_pass(k, first, source):
        arrived[k][q * PLANES + first] = source(q)[...]

        @pl.loop(1, PLANE)
        def _(p):
            reader = lax.rem(q + p, PLANE)
            send(source(reader), arrived[k].at[q * PLANES + first], xs.at[k], xr.at[k], z * PLANE + reader).start()

    def q_of(xx):
        return lax.rem(x + xx + 4, 4) * 2 + c

    def pieces_copy(k, i, qq, part, peer):
        piece = gathered[k].at[qq, part]
        return send(piece, piece, gs.at[k], gr.at[k * 15 + i], peer)

    def to_partner(k):
        return pieces_copy(k, 14, q, 1 - even, jnp.where(even == k % 2, up, down))

    def over_x(k, p):
        part = even if p else 1 - even
        return [pieces_copy(k, p * 7 + i, q, part, peer) for i, peer in enumerate((right, left))]

    def direct(k):
        return k >= PARTS - STRAIGHT

    def across(k, p):
        part, i = even if p else 1 - even, p * 7 + 2
        if direct(k):
            return pieces_copy(k, i, q, part, opposite)
        return pieces_copy(k, i, q_of(1 if p else -1), part, left if p else right)

    def to_core(k, p):
        part = even if p else 1 - even
        return [pieces_copy(k, p * 7 + 3 + i, q_of(xx), part, other) for i, xx in enumerate((0, -1, 1, 2))]

    def keep_own(k):
        part = pl.ds(PLANE * PLANES, own[k].shape[0])
        return pltpu.make_async_copy(features.at[:, pl.ds(k * part_rows, part_rows)], arrived[k].at[part], out_sem.at[k])

    def z_first(k):
        load(k).wait()
        z_start(k, 0)

    def all_blocks(k, count, sem):
        whole = arrived[k].at[pl.ds(0, count)]
        pltpu.make_async_copy(whole, whole, sem).wait()

    def plan_sent():
        most = rows_buf.at[pl.ds(0, PLANE - 1)]
        pltpu.make_async_copy(most, most, ps.at[0]).wait()
        for i in range(4):
            rows_copy(i).wait_send()

    def stage(k, s):
        if s == 0:
            if k == 0:
                z_first(0)
                share_plan()
                for part in range(PARTS):
                    if part == 1:
                        z_first(1)
                    elif part:
                        load(part).wait()
                    keep_own(part).start()
                    x_pick(part, 0, [(own[part], 0)])
            elif k > 1:
                z_start(k, 0)
        elif s == 1:
            z_wait(k, 0)
            z_start(k, 1)
            x_pick(k, 1, [(up1[k], -1), (down1[k], 1)])
        elif s == 2:
            z_wait(k, 1)
            if k == 0:
                take_plan()

            @pl.loop(0, PLANE)
            def _(reader):
                up3s[k][reader] = up2[k][block_of(1, reader, -2)]
                down3s[k][reader] = down2[k][block_of(-1, reader, 2)]

            @pl.loop(0, 4)
            def _(half):
                up3s[k][PLANE + half] = up2[k][block_of(2, 2 * half, -2)]
                down3s[k][PLANE + half] = down2[k][block_of(-2, 2 * half + 1, 2)]

            z_start(k, 2)
            x_pick(k, 3, [(up2[k], -2), (down2[k], 2)])
        elif s == 3:
            z_wait(k, 2)
            z_start(k, 3)
            x_pass(k, 5, lambda reader: up3[k].at[reader])
            x_pass(k, 6, lambda reader: down3[k].at[reader])
        elif s == 4:
            z_wait(k, 3)
            x_pass(k, 7, lambda reader: far[k].at[lax.rem(reader, 2), reader // 2])
        elif s == 5:
            all_blocks(k, (PLANE - 1) * PLANES, xr.at[k])
            keep_own(k).wait()
            for i in range(HEAVY):
                gathered[k][q, 1 - even, i] = arrived[k][table[me, 0, PLANES * PLANE + i]]
            for copy in [to_partner(k)] + over_x(k, 0) + [across(k, 0)] * direct(k) + to_core(k, 0)[:1]:
                copy.start()
            if k == 0:
                plan_sent()
        elif s == 6:
            to_partner(k).wait_recv()
            for copy in over_x(k, 1) + [across(k, 1)] * direct(k) + to_core(k, 1)[:1]:
                copy.start()
            for came in over_x(k, 0):
                came.wait_recv()
            for copy in [across(k, 0)] * (not direct(k)) + to_core(k, 0)[1:3]:
                copy.start()
        elif s == 7:
            for came in over_x(k, 1):
                came.wait_recv()
            for copy in [across(k, 1)] * (not direct(k)) + to_core(k, 1)[1:3]:
                copy.start()
            across(k, 0).wait_recv()
            to_core(k, 0)[3].start()
        elif s == 8:
            across(k, 1).wait_recv()
            to_core(k, 1)[3].start()
        elif s == 9:
            for copy in to_core(k, 0) + to_core(k, 1):
                copy.wait_recv()
            for sem in (zs.at[k], zs.at[PARTS + k]):
                all_blocks(k, 2 * own[k].shape[0] + PLANE + 8, sem)
            all_blocks(k, (PLANE - 1) * PLANES, xs.at[k])
            all_blocks(k, 15 * HEAVY, gs.at[k])

    for t in range(PARTS + 9):
        for s, lag in ORDER:
            if 0 <= t - lag < PARTS:
                stage(t - lag, s)
        for n in (2 * t, 2 * t + 1):
            if n * lot < tiles.shape[0]:
                split_tiles(n)


def exchange(cols, counts, own, tiles):
    blocks, side, feat = own.shape
    rows = side // PARTS
    vmem = pl.BlockSpec(memory_space=pltpu.VMEM)
    hbm = pl.BlockSpec(memory_space=pltpu.HBM)
    leads = [(blocks,)] * 5 + [(PLANE + 4,)] * 4 + [(2, 4), (PLANE, 5)]
    bufs = [pltpu.VMEM(lead + (rows, feat), jnp.float32) for lead in leads for _ in range(PARTS)]
    dma = pltpu.SemaphoreType.DMA
    return pl.pallas_call(
        exchange_kernel,
        out_shape=[jax.ShapeDtypeStruct((PLANE * PLANES + blocks, rows, feat), jnp.float32)] * PARTS
        + [jax.ShapeDtypeStruct((PLANE, 2, HEAVY, rows, feat), jnp.float32)] * PARTS
        + [jax.ShapeDtypeStruct((4, cols.shape[1]), jnp.int32)]
        + [jax.ShapeDtypeStruct(tiles.shape[:2] + (2 * tiles.shape[2],), jnp.bfloat16)],
        in_specs=[hbm] * 4,
        out_specs=[vmem] * (2 * PARTS + 2),
        scratch_shapes=bufs
        + [
            pltpu.VMEM((PLANE * PLANES, 1, cols.shape[1]), jnp.int32),
            pltpu.SMEM((PLANE * PLANES, 1, cols.shape[1]), jnp.int32),
            dma((PARTS,)),
            dma((PARTS * 2,)),
            dma((PARTS * 8,)),
            dma((PARTS,)),
            dma((PARTS,)),
            dma((PARTS,)),
            dma((PARTS * 15,)),
            dma((PARTS,)),
            dma((5,)),
            dma((5,)),
            dma((5,)),
            pltpu.VMEM((2, 8) + tiles.shape[1:], jnp.float32),
            dma((2,)),
            pltpu.VMEM(cols.shape, jnp.int32),
            pltpu.VMEM(counts.shape, jnp.int32),
            dma((2,)),
        ],
        compiler_params=pltpu.CompilerParams(collective_id=0, has_side_effects=True, vmem_limit_bytes=25 << 20),
    )(*(pltpu.with_memory_space_constraint(a, pltpu.HBM) for a in (cols, counts, own, tiles)))


def feat_sum_kernel(share, out, held, ss, rs):
    me, size = lax.axis_index("feat"), held.shape[0]
    peers = [lax.rem(me + p, size) for p in range(1, size)]
    barrier = pltpu.get_barrier_semaphore()
    for peer in peers:
        pl.semaphore_signal(barrier, inc=1, device_id={"feat": peer}, device_id_type=MESH)
    held[me] = share[...]
    pl.semaphore_wait(barrier, size - 1)
    copies = [
        pltpu.make_async_remote_copy(
            src_ref=held.at[me],
            dst_ref=held.at[me],
            send_sem=ss.at[i],
            recv_sem=rs.at[i],
            device_id={"feat": peer},
            device_id_type=MESH,
        )
        for i, peer in enumerate(peers)
    ]
    for copy in copies:
        copy.start()
    for copy in copies:
        copy.wait()
    out[...] = sum(held[i] for i in range(size))


def feat_sum(share):
    size = lax.axis_size("feat")
    vmem = pl.BlockSpec(memory_space=pltpu.VMEM)
    return pl.pallas_call(
        feat_sum_kernel,
        out_shape=jax.ShapeDtypeStruct(share.shape, jnp.float32),
        in_specs=[vmem],
        out_specs=vmem,
        scratch_shapes=[
            pltpu.VMEM((size,) + share.shape, jnp.float32),
            pltpu.SemaphoreType.DMA((size - 1,)),
            pltpu.SemaphoreType.DMA((size - 1,)),
        ],
        compiler_params=pltpu.CompilerParams(collective_id=1, has_side_effects=True, vmem_limit_bytes=2 << 20),
    )(share)


def per_device(features, norm_gain, row_counts, tile_cols, tile_values):
    node_dev, feat_dev = features.shape
    side = tile_values.shape[1]
    blocks = node_dev // side
    total = tile_values.shape[0]
    own = features.reshape(blocks, side, feat_dev)
    *blocks_got, plan, tiles = exchange(tile_cols.reshape(1, total), row_counts, own, tile_values)
    panel, heavy = blocks_got[:PARTS], [h.reshape((blocks * HEAVY,) + h.shape[-2:]) for h in blocks_got[PARTS:]]
    aggregate = tile_product(plan, tiles, panel, heavy)
    square_sum = feat_sum(jnp.sum(aggregate * aggregate, axis=2))
    mean_square = square_sum / (feat_dev * lax.axis_size("feat"))
    normed = aggregate * norm_gain[None, None, :] * lax.rsqrt(mean_square + 1e-05)[:, :, None]
    return normed.reshape(node_dev, feat_dev)


def solution(mesh):
    placed = (P("rows", "feat"), P("feat"), P("rows", None), P("rows"), P("rows", None, None))
    return jax.shard_map(
        per_device, mesh=mesh, in_specs=placed, out_specs=P("rows", "feat"), check_vma=False
    )
```
